512 devices in a mesh: gx: 64 (over x, z), gy: 8 (over y, core).
Axes of the slice: x: 4, y: 4, z: 16, core: 2. Of those that a mesh axis runs over, the one named last changes fastest.
Arguments:
- members: bfloat16 [128, 64, 128, 256], P('gx', 'gy'), may hold values from -6 to 6
- obs_pert: bfloat16 [8, 131072, 256], P('gy', 'gx'), may hold values from -6 to 6
- obs_weight: bfloat16 [8, 131072], P('gy', 'gx'), may hold values from 0.019897461 to 0.5
- obs_innov: bfloat16 [8, 131072], P('gy', 'gx'), may hold values from -12 to 12
- obs_node: int32 [8, 131072, 1], P('gy', 'gx'), may hold values from 0 to 63; in each aligned block of 2048 rows (0 to 2047, 2048 to 4095, ..., all dimensions but the last counted through in order) at most 48 rows name the same one
- neighbour_slot: int32 [4, 128, 64], P(None, 'gx', 'gy'), may hold values from 0 to 8
- interp_weight: float32 [4, 128, 64], P(None, 'gx', 'gy'), may hold values from 0.1 to 1
Outputs:
- analysis: bfloat16 [128, 64, 128, 256], P('gx', 'gy')
The draws below stay inside these ranges and needn't reach their ends.
Inputs may be any that keep to these rules, and one draw needn't show every extreme that they name: `obs_node`: within each device's aligned block of 2048 observations no node is named more than 48 times.
All inputs are finite; a program needn't handle non-finite values.
Results may differ from the reference program's by a relative error of at most 0.0063.
Values may be sent and summed in bfloat16 or wider, within the bound.
No kernel may reach another device: no remote copies, remote signals or barrier semaphores. Data moves between devices by JAX's collectives and lax.ppermute only.
A program may use at most 64 MiB of HBM per device.

```python
import math
import jax
import jax.numpy as jnp
import numpy as np
from jax import lax

K = 256
LEV = 128
CX = 2
CY = 8
OBS_DEV = 2048
NEWTON_STEPS = 8
CAP = 48
NCX = 128
NCY = 64
OBS_ROW = 131072
N_GX = 64
N_GY = 8


def place_ends(entries, rng, least, largest):
    longest = entries.shape.index(max(entries.shape))
    spots = []
    for shift in (0, 1):
        where = [jax.random.randint(jax.random.fold_in(rng, axis), (), 0, length) for axis, length in enumerate(entries.shape)]
        where[longest] = (where[longest] + shift) % entries.shape[longest]
        spots.append(tuple(where))
    return entries.at[spots[0]].set(least).at[spots[1]].set(largest)


def levels(stream_key, shape, cuts, smallest, top_value):
    def one(position, parts):
        steps = jax.random.uniform(jax.random.fold_in(jax.random.fold_in(stream_key, 6), position), (parts,), jnp.float32, smallest / len(cuts), top_value / len(cuts))
        return jnp.repeat(jnp.exp(steps), shape[position] // parts).reshape((-1,) + (1,) * (len(shape) - position - 1))

    loudness = one(*cuts[0])
    for cut in cuts[1:]:
        loudness = loudness * one(*cut)
    return loudness


def assign_block(own_key, own, number, rows, count, top, limit, slope):
    ranking = jax.random.permutation(own_key, count)
    heavy_load, ordinary = shares(count, rows * top, limit, slope, True), shares(count, rows * top, limit, slope, False)
    places = jnp.arange(count)

    def named(tallies, rotation):
        used = int((tallies > 0).sum())
        fixed = max(1, used // 4)
        shifted = fixed + (places - fixed + rotation * (used - fixed)) % max(1, count - fixed)
        return jnp.zeros((count,), jnp.int32).at[ranking[jnp.where(places < fixed, places, shifted)]].set(jnp.asarray(tallies, jnp.int32))

    tallies = jnp.where(number % 4 == 0, named(heavy_load, number // 4), named(ordinary, number - number // 4 - 1))
    mixed = jax.random.permutation(jax.random.fold_in(own, 3), count)
    giver, sink = mixed[0:count // 2 * 2:2], mixed[1:count // 2 * 2:2]
    room = jnp.minimum(tallies[giver] - 1, limit - tallies[sink]) // 2
    room = jnp.where((giver == ranking[0]) | (sink == ranking[0]) | (tallies[sink] == 0), 0, jnp.maximum(room, 0))
    shifted = jax.random.randint(jax.random.fold_in(own, 4), (count // 2,), 0, 1 << 20) % (room + 1)
    tallies = tallies.at[giver].add(-shifted).at[sink].add(shifted)
    items = jnp.searchsorted(jnp.cumsum(tallies), jnp.arange(rows * top), side="right").astype(jnp.int32)
    table = items.reshape(top, rows).T
    table = table[jax.random.permutation(jax.random.fold_in(own, 1), rows)]
    rotation = jax.random.randint(jax.random.fold_in(own, 2), (rows, 1), 0, top)
    return jnp.take_along_axis(table, (jnp.arange(top)[None, :] + rotation) % top, axis=1)


def shares(count, total, most, lean, full):
    weights = [(1 << 20) // math.isqrt(standing ** lean) + 1 for standing in range(1, count + 1)]
    largest = most if full else min(most, max(-(-total // count), total * weights[0] // sum(weights)))
    least = 1 if total - largest >= count - 1 else 0
    holding, rest = [largest] + [least] * (count - 1), total - largest - least * (count - 1)
    while rest > 0:
        free = [i for i in range(1, count) if holding[i] < largest] or [i for i in range(1, count) if holding[i] < most]
        pool, budget = sum([weights[i] for i in free]), rest
        for i in free:
            extra = min(most - holding[i], max(1, budget * weights[i] // pool), rest)
            holding[i] = holding[i] + extra
            rest = rest - extra
    return np.array(holding)


def noise(own_key, extent, deviation, reach, pieces=(), kind=jnp.bfloat16):
    result = jax.random.normal(own_key, extent, jnp.float32) * deviation
    if len(pieces) > 0:
        result = levels(own_key, extent, pieces, -0.22, 0.18) * result
    return jnp.clip(result, min=-reach, max=reach).astype(kind)


def setup_inputs(seed: int = 0) -> dict:
    streams_of = jax.random.split(jax.random.key(seed), 8)
    members = noise(streams_of[0], (NCX, NCY, LEV, K), 1.0, 6.0, ((0, 64), (1, 8)))
    obs_pert = noise(streams_of[1], (N_GY, OBS_ROW, K), 1.0, 6.0, ((0, 8), (1, 64)))
    obs_weight = jnp.clip(jnp.exp(math.log(0.5) - 3.224016 * jax.random.uniform(streams_of[2], (N_GY, OBS_ROW), jnp.float32) ** levels(streams_of[2], (N_GY, OBS_ROW), ((0, 8), (1, 64)), -0.2, 0.2)), 0.019897461, 0.5).astype(jnp.bfloat16)
    obs_innov = noise(streams_of[3], (N_GY, OBS_ROW), 2.0, 12.0, ((0, 8), (1, 64)))
    obs_node_keys = jax.random.split(jax.random.fold_in(streams_of[4], 1), N_GY * OBS_ROW // OBS_DEV)
    obs_node_turns = jax.random.permutation(jax.random.fold_in(streams_of[4], 3), N_GY * OBS_ROW // OBS_DEV)
    obs_node = jax.vmap(lambda own, number: assign_block(jax.random.fold_in(streams_of[4], 2), own, number, OBS_DEV, N_GX, 1, CAP, 2))(obs_node_keys, obs_node_turns).reshape((N_GY, OBS_ROW, 1))
    neighbour_slot = place_ends(jax.random.randint(streams_of[5], (4, NCX, NCY), 0, 9), jax.random.fold_in(streams_of[5], 1), 0, 8).astype(jnp.int32)
    interp_weight = jnp.clip(jnp.exp(math.log(1.0) - 2.3025851 * jax.random.uniform(streams_of[6], (4, NCX, NCY), jnp.float32) ** levels(streams_of[6], (4, NCX, NCY), ((1, 64), (2, 8)), -0.2, 0.2)), 0.1, 1.0)
    return {"members": members, "obs_pert": obs_pert, "obs_weight": obs_weight, "obs_innov": obs_innov, "obs_node": obs_node, "neighbour_slot": neighbour_slot, "interp_weight": interp_weight}


inflation = 1.1

def node_transform(pert, weight, innov):
    width = pert.shape[1]
    scaled = (pert.astype(jnp.float32) * weight.astype(jnp.float32)[:, None]).astype(jnp.bfloat16)
    gram = lax.dot_general(scaled, pert, (((0,), (0,)), ((), ())), preferred_element_type=jnp.float32)
    identity = jnp.eye(width, dtype=jnp.float32)
    gram = gram + (width - 1) / inflation * identity
    rhs = jnp.dot(innov[None, :], scaled, preferred_element_type=jnp.float32)[0]
    total = jnp.trace(gram)
    current_iterate = gram / total
    root = identity
    for step in range(NEWTON_STEPS):
        middle = 1.5 * identity - 0.5 * jnp.dot(root, current_iterate, precision=lax.Precision.HIGHEST)
        current_iterate = jnp.dot(current_iterate, middle, precision=lax.Precision.HIGHEST)
        root = jnp.dot(middle, root, precision=lax.Precision.HIGHEST)
    inverse = jnp.dot(root, root, precision=lax.Precision.HIGHEST) / total
    mean_weight = jnp.dot(inverse, rhs, precision=lax.Precision.HIGHEST)
    transform = mean_weight[:, None] + jnp.sqrt((width - 1) / total) * root
    return transform.astype(jnp.bfloat16)

def reference(members, obs_pert, obs_weight, obs_innov, obs_node, neighbour_slot, interp_weight):
    width = obs_pert.shape[2]
    capacity = 3 * OBS_DEV // (2 * N_GX)
    node_ids = jnp.arange(N_GX, dtype=jnp.int32)

    def build_row(args):
        pert, weight, innov, nodes = args
        block_tiles = nodes.reshape(N_GX, OBS_DEV)
        onehot = (block_tiles[:, :, None] == node_ids[None, None, :]).astype(jnp.int32)
        rank = lax.optimization_barrier(jnp.sum(jnp.cumsum(onehot, 1) * onehot, 2)) - 1
        source = node_ids[:, None]
        flat = ((block_tiles * N_GX + source) * capacity + rank).reshape(-1).astype(jnp.int32)
        count = N_GX * N_GX * capacity
        bpert = jnp.zeros((count, width), jnp.bfloat16).at[flat].set(pert).reshape(N_GX, N_GX * capacity, width)
        bweight = jnp.zeros((count,), jnp.bfloat16).at[flat].set(weight).reshape(N_GX, N_GX * capacity)
        binnov = jnp.zeros((count,), jnp.bfloat16).at[flat].set(innov).reshape(N_GX, N_GX * capacity)
        return lax.map(lambda item: node_transform(item[0], item[1], item[2]), (bpert, bweight, binnov))
    by_row = lax.map(build_row, (obs_pert, obs_weight, obs_innov, obs_node[:, :, 0]))
    transforms = jnp.transpose(by_row, (1, 0, 2, 3))
    column_x = jnp.arange(NCX, dtype=jnp.int32)[:, None]
    column_coord_y = jnp.arange(NCY, dtype=jnp.int32)[None, :]
    node_coord_x = (column_x // CX + neighbour_slot // 3 - 1) % N_GX
    node_y = (column_coord_y // CY + neighbour_slot % 3 - 1) % N_GY
    share = interp_weight / lax.optimization_barrier(jnp.sum(interp_weight, 0))

    def column_row(args):
        state, along_x, along_y, part = args
        picked = transforms[along_x, along_y].astype(jnp.float32)
        blend_factor = lax.optimization_barrier(jnp.sum(part[:, :, None, None] * picked, 0)).astype(jnp.bfloat16)
        mean = lax.optimization_barrier(jnp.mean(state.astype(jnp.float32), -1))
        member_anomaly = (state.astype(jnp.float32) - mean[..., None]).astype(jnp.bfloat16)
        update_matrix = jnp.einsum('frt,fty->fry', member_anomaly.astype(jnp.float32), blend_factor.astype(jnp.float32))
        return (mean[..., None] + update_matrix).astype(jnp.bfloat16)
    return lax.map(column_row, (members, jnp.moveaxis(node_coord_x, 1, 0), jnp.moveaxis(node_y, 1, 0), jnp.moveaxis(share, 1, 0)))
```

```python
import jax
import jax.numpy as jnp
from jax import lax
from jax.experimental import pallas as pl
from jax.experimental.pallas import tpu as pltpu
from jax.sharding import Mesh
from jax.sharding import PartitionSpec as P

NEWTON_STEPS = 8
inflation = 1.1

SHAPE = (4, 8, 2, 4, 2)
AXES = ("x", "zh", "zl", "y", "c")
GX = ("x", "zh", "zl")
GY = ("y", "c")

NODES = 64
HIGH = 8
GROUP = 8
CAP = 48
OBS = 2048
K = 256
HALF = 128
ROWS = HIGH * CAP + 16
PACKED = K + 8
WIRE = jnp.bfloat16
F32 = jnp.float32
BF16 = jnp.bfloat16


def iota(shape, dim):
    return lax.broadcasted_iota(jnp.int32, shape, dim)


def route_kernel(node_ref, weight_ref, innov_ref, pert_ref, out_ref, rank_ref, scaled_ref, rhs_ref):
    step = pl.program_id(0)

    @pl.when(step == 0)
    def _():
        row = iota((NODES, 1), 0)
        name = (row // 16) * 16 + (row % 8) * 2 + (row // 8) % 2
        onehot = (node_ref[...] == name).astype(F32)
        upper = (iota((K, K), 0) <= iota((K, K), 1)).astype(BF16)
        carry = jnp.zeros((NODES, 1), F32)
        for b in range(OBS // K):
            part = onehot[:, b * K : (b + 1) * K]
            count = jnp.dot(part.astype(BF16), upper, preferred_element_type=F32) + carry
            rank_ref[:, b * K : (b + 1) * K] = jnp.where(part > 0, count - 1.0, -1.0)
            carry = count[:, K - 1 : K]
        weight = weight_ref[...].astype(F32)
        side = jnp.sqrt(weight)
        side = jnp.concatenate([side[:, k * 128 : (k + 1) * 128] for k in range(OBS // 128)], 0).T
        for k in range(OBS // 128):
            rows = pl.ds(k * 128, 128)
            scaled_ref[rows, :] = (pert_ref[rows, :].astype(F32) * side[:, k : k + 1]).astype(BF16)
        factor = onehot * (weight * innov_ref[...].astype(F32))
        top = factor.astype(BF16)
        rest = (factor - top.astype(F32)).astype(BF16)
        both = jnp.dot(jnp.concatenate([top, rest], 0), pert_ref[...], preferred_element_type=F32)
        rhs_ref[...] = both[:NODES] + both[NODES:]

    rank = rank_ref[pl.ds(pl.multiple_of(step * HIGH, HIGH), HIGH), :]
    wanted = iota((CAP, OBS), 0).astype(F32)
    pick = jnp.concatenate([(rank[h : h + 1, :] == wanted).astype(BF16) for h in range(HIGH)], 0)
    out_ref[0, : HIGH * CAP, :] = jnp.dot(
        pick, scaled_ref[...], preferred_element_type=F32
    ).astype(BF16)
    rhs = rhs_ref[pl.ds(pl.multiple_of(step * HIGH, HIGH), HIGH), :]
    top = rhs.astype(BF16).astype(F32)
    out_ref[0, HIGH * CAP :, :] = jnp.concatenate([top, rhs - top], 0).astype(BF16)


def route(node, weight, innov, pert):
    whole = lambda shape: pl.BlockSpec(shape, lambda d: (0, 0))
    return pl.pallas_call(
        route_kernel,
        grid=(GROUP,),
        in_specs=[whole((1, OBS)), whole((1, OBS)), whole((1, OBS)), whole((OBS, K))],
        out_specs=pl.BlockSpec((1, ROWS, K), lambda d: (d, 0, 0)),
        out_shape=jax.ShapeDtypeStruct((GROUP, ROWS, K), BF16),
        scratch_shapes=[
            pltpu.VMEM((NODES, OBS), F32),
            pltpu.VMEM((OBS, K), BF16),
            pltpu.VMEM((NODES, K), F32),
        ],
        name="route",
    )(node, weight, innov, pert)


def gram_kernel(obs_ref, side_ref, out_ref):
    step = pl.program_id(0)
    obs = obs_ref[...].reshape(GROUP * CAP, K)
    gram = lax.dot_general(obs, obs, (((0,), (0,)), ((), ())), preferred_element_type=F32)
    first, cross, last = gram[:HALF, :HALF], gram[:HALF, HALF:], gram[HALF:, HALF:]
    low, high = iota((HALF, HALF), 0), iota((HALF, HALF), 1)
    eye = low == high
    first_diag = jnp.sum(jnp.where(eye, first, 0.0), 0, keepdims=True)
    last_diag = jnp.sum(jnp.where(eye, last, 0.0), 0, keepdims=True)
    sides = jnp.sum(side_ref[...].astype(F32), 0)
    mine = iota((16, K), 0) % HIGH == step
    rhs = jnp.sum(jnp.where(mine, sides, 0.0), 0, keepdims=True)
    out_ref[0, :HALF, :] = jnp.where(low <= high, first, last).astype(WIRE)
    out_ref[0, HALF:K, :] = cross.astype(WIRE)
    rest = lambda v: v - v.astype(WIRE).astype(F32)
    extra = jnp.concatenate(
        [
            last_diag,
            rest(last_diag),
            rest(first_diag),
            rhs[:, :HALF],
            rhs[:, HALF:],
            rest(rhs[:, :HALF]),
            rest(rhs[:, HALF:]),
            jnp.zeros((1, HALF), F32),
        ],
        0,
    )
    out_ref[0, K:, :] = extra.astype(WIRE)


def partial_grams(got):
    return pl.pallas_call(
        gram_kernel,
        grid=(HIGH,),
        in_specs=[
            pl.BlockSpec((GROUP, CAP, K), lambda h: (0, h, 0)),
            pl.BlockSpec((GROUP, 16, K), lambda h: (0, HIGH * CAP // 16, 0)),
        ],
        out_specs=pl.BlockSpec((1, PACKED, HALF), lambda h: (h, 0, 0)),
        out_shape=jax.ShapeDtypeStruct((HIGH, PACKED, HALF), WIRE),
        name="gram",
    )(got, got)


def split(a):
    top = a.astype(BF16)
    return top, (a - top.astype(F32)).astype(BF16)


def dot3(a, b):
    (a_top, a_rest), (b_top, b_rest) = a, b
    dot = lambda u, v: jnp.dot(u, v, preferred_element_type=F32)
    return dot(a_top, b_top) + (dot(a_top, b_rest) + dot(a_rest, b_top))


def newton_kernel(got_ref, out_ref):
    packed = jnp.sum(got_ref[...].astype(F32), 0)
    mixed, cross, extra = packed[:HALF], packed[HALF:K], packed[K:]
    low, high = iota((HALF, HALF), 0), iota((HALF, HALF), 1)
    eye = low == high
    base = (K - 1) / inflation
    upper = jnp.where(low < high, mixed, 0.0)
    lower = jnp.where(low > high, mixed, 0.0)
    first_diag = jnp.where(eye, mixed + extra[2:3] + base, 0.0)
    last_diag = jnp.where(eye, extra[0:1] + extra[1:2] + base, 0.0)
    first = upper + upper.T + first_diag
    last = lower + lower.T + last_diag
    gram = jnp.concatenate(
        [jnp.concatenate([first, cross], 1), jnp.concatenate([cross.T, last], 1)], 0
    )
    rhs = jnp.concatenate([extra[3:4] + extra[5:6], extra[4:5] + extra[6:7]], 1)
    total = jnp.sum(jnp.sum(first_diag + last_diag, 1, keepdims=True), 0, keepdims=True)
    identity = (iota((K, K), 0) == iota((K, K), 1)).astype(F32)
    error = gram / total
    root = None
    for step in range(NEWTON_STEPS):
        middle = 1.5 * identity - 0.5 * error
        middle_parts = split(middle)
        root = middle if step == 0 else dot3(split(root), middle_parts)
        if step < NEWTON_STEPS - 1:
            error = dot3(split(error), middle_parts)
            error = dot3(split(error), middle_parts)
    once = jnp.dot(
        jnp.broadcast_to(rhs, (8, K)), root, precision=lax.Precision.HIGHEST, preferred_element_type=F32
    )[:1]
    mean_weight = jnp.sum(root * once, 1, keepdims=True) / total
    out_ref[...] = (mean_weight + jnp.sqrt((K - 1) / total) * root).astype(BF16)


def node_transform(got):
    return pl.pallas_call(
        newton_kernel,
        out_shape=jax.ShapeDtypeStruct((K, K), BF16),
        name="newton",
    )(got)


def analysis_kernel(slot_ref, share_ref, table_ref, state_ref, out_ref):
    step = pl.program_id(0)
    for n in range(COLS):
        column = step * COLS + n
        blend = share_ref[0, column] * table_ref[slot_ref[0, column]].astype(F32)
        for q in range(1, 4):
            blend += share_ref[q, column] * table_ref[slot_ref[q, column]].astype(F32)
        state = state_ref[n].astype(F32)
        mean = jnp.mean(state, -1, keepdims=True)
        anomaly = (state - mean).astype(BF16)
        update = jnp.dot(anomaly, blend.astype(BF16), preferred_element_type=F32)
        out_ref[n] = (mean + update).astype(BF16)


COLS = 4


def analyse(slots, share, table, state):
    columns, levels, width = state.shape
    block = pl.BlockSpec((COLS, levels, width), lambda f, *_: (f, 0, 0))
    return pl.pallas_call(
        analysis_kernel,
        grid_spec=pltpu.PrefetchScalarGridSpec(
            num_scalar_prefetch=2,
            grid=(columns // COLS,),
            in_specs=[pl.BlockSpec((9, K, K), lambda f, *_: (0, 0, 0)), block],
            out_specs=block,
        ),
        out_shape=jax.ShapeDtypeStruct(state.shape, BF16),
        name="analysis",
    )(slots, share, table, state)


def swap(block, axes, count):
    even = [(i, i ^ 1) for i in range(count)]
    odd = [(i, (((i + 1) ^ 1) - 1) % count) for i in range(count)]
    return lax.ppermute(block, axes, even), lax.ppermute(block, axes, odd)


def shards(members, obs_pert, obs_weight, obs_innov, obs_node, neighbour_slot, interp_weight):
    sent = route(obs_node.reshape(1, OBS), obs_weight, obs_innov, obs_pert[0])
    got = lax.all_to_all(sent, ("x", "zl"), split_axis=0, concat_axis=0, tiled=True)
    grams = partial_grams(got)
    grams = lax.all_to_all(grams, "zh", split_axis=0, concat_axis=0, tiled=True)
    own = node_transform(grams)
    even, odd = swap(own, GX, 64)
    line = jnp.stack([even, own, odd])
    even, odd = swap(line, GY, 8)
    table = jnp.concatenate([even, line, odd])
    columns = members.shape[0] * members.shape[1]
    slots = neighbour_slot.reshape(4, columns)
    share = interp_weight.reshape(4, columns)
    share = share / jnp.sum(share, 0)

    def place(offset, axes):
        flip = lax.axis_index(axes) % 2 == 1
        return jnp.where(flip, offset, 2 - offset)

    slots = place(slots % 3, GY) * 3 + place(slots // 3, GX)
    state = members.reshape(columns, *members.shape[2:])
    return analyse(slots, share, table, state).reshape(members.shape)


def solution(mesh):
    fine = Mesh(mesh.devices.reshape(SHAPE), AXES)
    return jax.shard_map(
        shards,
        mesh=fine,
        in_specs=(
            P(GX, GY, None, None),
            P(GY, GX, None),
            P(GY, GX),
            P(GY, GX),
            P(GY, GX, None),
            P(None, GX, GY),
            P(None, GX, GY),
        ),
        out_specs=P(GX, GY, None, None),
        check_vma=False,
    )
```

```python
import jax
import jax.numpy as jnp
from jax import lax
from jax.experimental import pallas as pl
from jax.experimental.pallas import tpu as pltpu
from jax.sharding import Mesh
from jax.sharding import PartitionSpec as P

NEWTON_STEPS = 8
inflation = 1.1

SHAPE = (4, 8, 2, 4, 2)
AXES = ("x", "zh", "zl", "y", "c")
GX = ("x", "zh", "zl")
GY = ("y", "c")

NODES = 64
HIGH = 8
GROUP = 8
CAP = 48
OBS = 2048
K = 256
HALF = 128
ROWS = HIGH * CAP + 16
PACKED = K + 8
WIRE = jnp.bfloat16
F32 = jnp.float32
BF16 = jnp.bfloat16


def iota(shape, dim):
    return lax.broadcasted_iota(jnp.int32, shape, dim)


def route_kernel(node_ref, weight_ref, innov_ref, pert_ref, out_ref, rank_ref, scaled_ref, rhs_ref):
    step = pl.program_id(0)

    @pl.when(step == 0)
    def _():
        row = iota((NODES, 1), 0)
        name = (row // 16) * 16 + (row % 8) * 2 + (row // 8) % 2
        onehot = (node_ref[...] == name).astype(F32)
        upper = (iota((K, K), 0) <= iota((K, K), 1)).astype(BF16)
        carry = jnp.zeros((NODES, 1), F32)
        for b in range(OBS // K):
            part = onehot[:, b * K : (b + 1) * K]
            count = jnp.dot(part.astype(BF16), upper, preferred_element_type=F32) + carry
            rank_ref[:, b * K : (b + 1) * K] = jnp.where(part > 0, count - 1.0, -1.0)
            carry = count[:, K - 1 : K]
        weight = weight_ref[...].astype(F32)
        side = jnp.sqrt(weight)
        side = jnp.concatenate([side[:, k * 128 : (k + 1) * 128] for k in range(OBS // 128)], 0).T
        for k in range(OBS // 128):
            rows = pl.ds(k * 128, 128)
            scaled_ref[rows, :] = (pert_ref[rows, :].astype(F32) * side[:, k : k + 1]).astype(BF16)
        factor = onehot * (weight * innov_ref[...].astype(F32))
        top = factor.astype(BF16)
        rest = (factor - top.astype(F32)).astype(BF16)
        both = jnp.dot(jnp.concatenate([top, rest], 0), pert_ref[...], preferred_element_type=F32)
        rhs_ref[...] = both[:NODES] + both[NODES:]

    rank = rank_ref[pl.ds(pl.multiple_of(step * HIGH, HIGH), HIGH), :]
    wanted = iota((CAP, OBS), 0).astype(F32)
    pick = jnp.concatenate([(rank[h : h + 1, :] == wanted).astype(BF16) for h in range(HIGH)], 0)
    out_ref[0, : HIGH * CAP, :] = jnp.dot(
        pick, scaled_ref[...], preferred_element_type=F32
    ).astype(BF16)
    rhs = rhs_ref[pl.ds(pl.multiple_of(step * HIGH, HIGH), HIGH), :]
    top = rhs.astype(BF16).astype(F32)
    out_ref[0, HIGH * CAP :, :] = jnp.concatenate([top, rhs - top], 0).astype(BF16)


def route(node, weight, innov, pert):
    whole = lambda shape: pl.BlockSpec(shape, lambda d: (0, 0))
    return pl.pallas_call(
        route_kernel,
        grid=(GROUP,),
        in_specs=[whole((1, OBS)), whole((1, OBS)), whole((1, OBS)), whole((OBS, K))],
        out_specs=pl.BlockSpec((1, ROWS, K), lambda d: (d, 0, 0)),
        out_shape=jax.ShapeDtypeStruct((GROUP, ROWS, K), BF16),
        scratch_shapes=[
            pltpu.VMEM((NODES, OBS), F32),
            pltpu.VMEM((OBS, K), BF16),
            pltpu.VMEM((NODES, K), F32),
        ],
        name="route",
        compiler_params=pltpu.CompilerParams(vmem_limit_bytes=40 << 20),
    )(node, weight, innov, pert)


PER = 2


def gram_kernel(obs_ref, side_ref, out_ref):
    step = pl.program_id(0)
    low, high = iota((HALF, HALF), 0), iota((HALF, HALF), 1)
    eye = low == high
    keep = low <= high
    rest = lambda v: v - v.astype(WIRE).astype(F32)
    sides = jnp.sum(side_ref[...].astype(F32), 0)
    name = iota((16, K), 0) % HIGH
    for n in range(PER):
        obs = obs_ref[:, n * CAP : (n + 1) * CAP, :].reshape(GROUP * CAP, K)
        gram = lax.dot_general(obs, obs, (((0,), (0,)), ((), ())), preferred_element_type=F32)
        first, cross, last = gram[:HALF, :HALF], gram[:HALF, HALF:], gram[HALF:, HALF:]
        first_diag = jnp.sum(jnp.where(eye, first, 0.0), 0, keepdims=True)
        last_diag = jnp.sum(jnp.where(eye, last, 0.0), 0, keepdims=True)
        rhs = jnp.sum(jnp.where(name == step * PER + n, sides, 0.0), 0, keepdims=True)
        out_ref[n, :HALF, :] = jnp.where(keep, first, last).astype(WIRE)
        out_ref[n, HALF:K, :] = cross.astype(WIRE)
        extra = jnp.concatenate(
            [
                last_diag,
                rest(last_diag),
                rest(first_diag),
                rhs[:, :HALF],
                rhs[:, HALF:],
                rest(rhs[:, :HALF]),
                rest(rhs[:, HALF:]),
                jnp.zeros((1, HALF), F32),
            ],
            0,
        )
        out_ref[n, K:, :] = extra.astype(WIRE)


def partial_grams(got):
    return pl.pallas_call(
        gram_kernel,
        grid=(HIGH // PER,),
        in_specs=[
            pl.BlockSpec((GROUP, PER * CAP, K), lambda h: (0, h, 0)),
            pl.BlockSpec((GROUP, 16, K), lambda h: (0, HIGH * CAP // 16, 0)),
        ],
        out_specs=pl.BlockSpec((PER, PACKED, HALF), lambda h: (h, 0, 0)),
        out_shape=jax.ShapeDtypeStruct((HIGH, PACKED, HALF), WIRE),
        name="gram",
        compiler_params=pltpu.CompilerParams(vmem_limit_bytes=16 << 20),
    )(got, got)


def split(a):
    top = a.astype(BF16)
    return top, (a - top.astype(F32)).astype(BF16)


def dot3(a, b):
    (a_top, a_rest), (b_top, b_rest) = a, b
    dot = lambda u, v: jnp.dot(u, v, preferred_element_type=F32)
    return dot(a_top, b_top) + (dot(a_top, b_rest) + dot(a_rest, b_top))


def newton_kernel(got_ref, out_ref):
    packed = jnp.sum(got_ref[...].astype(F32), 0)
    mixed, cross, extra = packed[:HALF], packed[HALF:K], packed[K:]
    low, high = iota((HALF, HALF), 0), iota((HALF, HALF), 1)
    eye = low == high
    base = (K - 1) / inflation
    upper = jnp.where(low < high, mixed, 0.0)
    lower = jnp.where(low > high, mixed, 0.0)
    first_diag = jnp.where(eye, mixed + extra[2:3] + base, 0.0)
    last_diag = jnp.where(eye, extra[0:1] + extra[1:2] + base, 0.0)
    first = upper + upper.T + first_diag
    last = lower + lower.T + last_diag
    gram = jnp.concatenate(
        [jnp.concatenate([first, cross], 1), jnp.concatenate([cross.T, last], 1)], 0
    )
    rhs = jnp.concatenate([extra[3:4] + extra[5:6], extra[4:5] + extra[6:7]], 1)
    total = jnp.sum(jnp.sum(first_diag + last_diag, 1, keepdims=True), 0, keepdims=True)
    identity = (iota((K, K), 0) == iota((K, K), 1)).astype(F32)
    error = gram / total
    root = None
    for step in range(NEWTON_STEPS - 1):
        top, rest = split(error)
        half = (0.5 * error).astype(BF16)
        dot = lambda u: jnp.dot(u, half, preferred_element_type=F32)
        if step == 0:
            root = 1.5 * identity - half.astype(F32)
        else:
            root_top, root_rest = split(root)
            root = 1.5 * root - (dot(root_top) + dot(root_rest))
        error = 1.5 * error - (dot(top) + dot(rest))
        top, rest = split(error)
        error = 1.5 * error - (dot(top) + dot(rest))
    root = 1.5 * root - 0.5 * dot3(split(root), split(error))
    once = jnp.dot(
        jnp.broadcast_to(rhs, (8, K)), root, precision=lax.Precision.HIGHEST, preferred_element_type=F32
    )[:1]
    mean_weight = jnp.sum(root * once, 1, keepdims=True) / total
    out_ref[...] = (mean_weight + jnp.sqrt((K - 1) / total) * root).astype(BF16)


def node_transform(got):
    return pl.pallas_call(
        newton_kernel,
        out_shape=jax.ShapeDtypeStruct((K, K), BF16),
        name="newton",
        compiler_params=pltpu.CompilerParams(vmem_limit_bytes=12 << 20),
    )(got)


def analysis_kernel(slot_ref, share_ref, flip_ref, table_ref, state_ref, out_ref):
    step = pl.program_id(0)
    flip_x, flip_y = flip_ref[0], flip_ref[1]
    for n in range(COLS):
        column = step * COLS + n
        cx, cy = column // CY, column % CY
        total = 0.0
        blend = None
        for q in range(4):
            slot = slot_ref[q, cx, cy]
            ox, oy = slot // 3, slot % 3
            ox = jnp.where(flip_x == 1, ox, 2 - ox)
            oy = jnp.where(flip_y == 1, oy, 2 - oy)
            share = share_ref[q, cx, cy]
            total += share
            term = share * table_ref[oy * 3 + ox].astype(F32)
            blend = term if q == 0 else blend + term
        blend = blend / jnp.full((1, 1), total, F32)
        state = state_ref[n].astype(F32)
        mean = jnp.mean(state, -1, keepdims=True)
        anomaly = (state - mean).astype(BF16)
        update = jnp.dot(anomaly, blend.astype(BF16), preferred_element_type=F32)
        out_ref[n] = (mean + update).astype(BF16)


CX = 2
CY = 8
COLS = 4


def analyse(slots, share, flips, table, state):
    columns, levels, width = state.shape
    block = pl.BlockSpec((COLS, levels, width), lambda f, *_: (f, 0, 0))
    return pl.pallas_call(
        analysis_kernel,
        grid_spec=pltpu.PrefetchScalarGridSpec(
            num_scalar_prefetch=3,
            grid=(columns // COLS,),
            in_specs=[pl.BlockSpec((9, K, K), lambda f, *_: (0, 0, 0)), block],
            out_specs=block,
        ),
        out_shape=jax.ShapeDtypeStruct(state.shape, BF16),
        name="analysis",
        compiler_params=pltpu.CompilerParams(vmem_limit_bytes=16 << 20),
    )(slots, share, flips, table, state)


def swap(block, axes, count):
    even = [(i, i ^ 1) for i in range(count)]
    odd = [(i, (((i + 1) ^ 1) - 1) % count) for i in range(count)]
    return lax.ppermute(block, axes, even), lax.ppermute(block, axes, odd)


def shards(members, obs_pert, obs_weight, obs_innov, obs_node, neighbour_slot, interp_weight):
    sent = route(obs_node.reshape(1, OBS), obs_weight, obs_innov, obs_pert[0])
    got = lax.all_to_all(sent, ("x", "zl"), split_axis=0, concat_axis=0, tiled=True)
    grams = partial_grams(got)
    grams = lax.all_to_all(grams, "zh", split_axis=0, concat_axis=0, tiled=True)
    own = node_transform(grams)
    even, odd = swap(own, GX, 64)
    line = jnp.stack([even, own, odd])
    even, odd = swap(line, GY, 8)
    table = jnp.concatenate([even, line, odd])
    flips = jnp.stack([lax.axis_index(GX) % 2, lax.axis_index(GY) % 2]).astype(jnp.int32)
    state = members.reshape(CX * CY, *members.shape[2:])
    return analyse(neighbour_slot, interp_weight, flips, table, state).reshape(members.shape)


def solution(mesh):
    fine = Mesh(mesh.devices.reshape(SHAPE), AXES)
    return jax.shard_map(
        shards,
        mesh=fine,
        in_specs=(
            P(GX, GY, None, None),
            P(GY, GX, None),
            P(GY, GX),
            P(GY, GX),
            P(GY, GX, None),
            P(None, GX, GY),
            P(None, GX, GY),
        ),
        out_specs=P(GX, GY, None, None),
        check_vma=False,
    )
```

```python
import jax
import jax.numpy as jnp
from jax import lax
from jax.experimental import pallas as pl
from jax.experimental.pallas import tpu as pltpu
from jax.sharding import Mesh
from jax.sharding import PartitionSpec as P

NEWTON_STEPS = 8
inflation = 1.1

SHAPE = (4, 8, 2, 4, 2)
AXES = ("x", "zh", "zl", "y", "c")
GX = ("x", "zh", "zl")
GY = ("y", "c")

NODES = 64
HIGH = 8
GROUP = 8
CAP = 48
OBS = 2048
K = 256
HALF = 128
ROWS = HIGH * CAP + 16
PACKED = K + 8
WIRE = jnp.bfloat16
F32 = jnp.float32
BF16 = jnp.bfloat16


def iota(shape, dim):
    return lax.broadcasted_iota(jnp.int32, shape, dim)


def route_kernel(
    node_hbm, weight_hbm, innov_hbm, pert_hbm, out_ref,
    rank_ref, scaled_ref, rhs_ref, node_ref, weight_ref, innov_ref, pert_ref, sems,
):
    step = pl.program_id(0)

    @pl.when(step == 0)
    def _():
        pairs = (
            (node_hbm, node_ref), (pert_hbm, pert_ref), (weight_hbm, weight_ref), (innov_hbm, innov_ref),
        )
        copies = [pltpu.make_async_copy(a, b, sems.at[i]) for i, (a, b) in enumerate(pairs)]
        for copy in copies:
            copy.start()
        copies[0].wait()
        row = iota((NODES, 1), 0)
        name = (row // 16) * 16 + (row % 8) * 2 + (row // 8) % 2
        onehot = (node_ref[...] == name).astype(F32)
        upper = (iota((K, K), 0) <= iota((K, K), 1)).astype(BF16)
        carry = jnp.zeros((NODES, 1), F32)
        for b in range(OBS // K):
            part = onehot[:, b * K : (b + 1) * K]
            count = jnp.dot(part.astype(BF16), upper, preferred_element_type=F32) + carry
            rank_ref[:, b * K : (b + 1) * K] = jnp.where(part > 0, count - 1.0, -1.0)
            carry = count[:, K - 1 : K]
        for copy in copies[1:]:
            copy.wait()
        weight = weight_ref[...].astype(F32)
        side = jnp.sqrt(weight)
        side = jnp.concatenate([side[:, k * 128 : (k + 1) * 128] for k in range(OBS // 128)], 0).T
        for k in range(OBS // 128):
            rows = pl.ds(k * 128, 128)
            scaled_ref[rows, :] = (pert_ref[rows, :].astype(F32) * side[:, k : k + 1]).astype(BF16)
        factor = onehot * (weight * innov_ref[...].astype(F32))
        top = factor.astype(BF16)
        rest = (factor - top.astype(F32)).astype(BF16)
        both = jnp.dot(jnp.concatenate([top, rest], 0), pert_ref[...], preferred_element_type=F32)
        rhs_ref[...] = both[:NODES] + both[NODES:]

    rank = rank_ref[pl.ds(pl.multiple_of(step * HIGH, HIGH), HIGH), :]
    wanted = iota((CAP, OBS), 0).astype(F32)
    pick = jnp.concatenate([(rank[h : h + 1, :] == wanted).astype(BF16) for h in range(HIGH)], 0)
    out_ref[0, : HIGH * CAP, :] = jnp.dot(
        pick, scaled_ref[...], preferred_element_type=F32
    ).astype(BF16)
    rhs = rhs_ref[pl.ds(pl.multiple_of(step * HIGH, HIGH), HIGH), :]
    top = rhs.astype(BF16).astype(F32)
    out_ref[0, HIGH * CAP :, :] = jnp.concatenate([top, rhs - top], 0).astype(BF16)


def route(node, weight, innov, pert):
    return pl.pallas_call(
        route_kernel,
        grid=(GROUP,),
        in_specs=[pl.BlockSpec(memory_space=pltpu.HBM)] * 4,
        out_specs=pl.BlockSpec((1, ROWS, K), lambda d: (d, 0, 0)),
        out_shape=jax.ShapeDtypeStruct((GROUP, ROWS, K), BF16),
        scratch_shapes=[
            pltpu.VMEM((NODES, OBS), F32),
            pltpu.VMEM((OBS, K), BF16),
            pltpu.VMEM((NODES, K), F32),
            pltpu.VMEM((1, OBS), jnp.int32),
            pltpu.VMEM((1, OBS), BF16),
            pltpu.VMEM((1, OBS), BF16),
            pltpu.VMEM((OBS, K), BF16),
            pltpu.SemaphoreType.DMA((4,)),
        ],
        name="route",
        compiler_params=pltpu.CompilerParams(vmem_limit_bytes=40 << 20),
    )(*[pltpu.with_memory_space_constraint(v, pltpu.HBM) for v in (node, weight, innov, pert)])


PER = 2


def gram_kernel(obs_ref, side_ref, out_ref):
    step = pl.program_id(0)
    low, high = iota((HALF, HALF), 0), iota((HALF, HALF), 1)
    eye = low == high
    keep = low <= high
    rest = lambda v: v - v.astype(WIRE).astype(F32)
    sides = jnp.sum(side_ref[...].astype(F32), 0)
    name = iota((16, K), 0) % HIGH
    for n in range(PER):
        obs = obs_ref[:, n * CAP : (n + 1) * CAP, :].reshape(GROUP * CAP, K)
        gram = lax.dot_general(obs, obs, (((0,), (0,)), ((), ())), preferred_element_type=F32)
        first, cross, last = gram[:HALF, :HALF], gram[:HALF, HALF:], gram[HALF:, HALF:]
        first_diag = jnp.sum(jnp.where(eye, first, 0.0), 0, keepdims=True)
        last_diag = jnp.sum(jnp.where(eye, last, 0.0), 0, keepdims=True)
        rhs = jnp.sum(jnp.where(name == step * PER + n, sides, 0.0), 0, keepdims=True)
        out_ref[n, :HALF, :] = jnp.where(keep, first, last).astype(WIRE)
        out_ref[n, HALF:K, :] = cross.astype(WIRE)
        extra = jnp.concatenate(
            [
                last_diag,
                rest(last_diag),
                rest(first_diag),
                rhs[:, :HALF],
                rhs[:, HALF:],
                rest(rhs[:, :HALF]),
                rest(rhs[:, HALF:]),
                jnp.zeros((1, HALF), F32),
            ],
            0,
        )
        out_ref[n, K:, :] = extra.astype(WIRE)


def partial_grams(got):
    return pl.pallas_call(
        gram_kernel,
        grid=(HIGH // PER,),
        in_specs=[
            pl.BlockSpec((GROUP, PER * CAP, K), lambda h: (0, h, 0)),
            pl.BlockSpec((GROUP, 16, K), lambda h: (0, HIGH * CAP // 16, 0)),
        ],
        out_specs=pl.BlockSpec((PER, PACKED, HALF), lambda h: (h, 0, 0)),
        out_shape=jax.ShapeDtypeStruct((HIGH, PACKED, HALF), WIRE),
        name="gram",
        compiler_params=pltpu.CompilerParams(vmem_limit_bytes=16 << 20),
    )(got, got)


def split(a):
    top = a.astype(BF16)
    return top, (a - top.astype(F32)).astype(BF16)


def dot3(a, b):
    (a_top, a_rest), (b_top, b_rest) = a, b
    dot = lambda u, v: jnp.dot(u, v, preferred_element_type=F32)
    return dot(a_top, b_top) + (dot(a_top, b_rest) + dot(a_rest, b_top))


def newton_kernel(got_ref, out_ref):
    packed = jnp.sum(got_ref[...].astype(F32), 0)
    mixed, cross, extra = packed[:HALF], packed[HALF:K], packed[K:]
    low, high = iota((HALF, HALF), 0), iota((HALF, HALF), 1)
    eye = low == high
    base = (K - 1) / inflation
    upper = jnp.where(low < high, mixed, 0.0)
    lower = jnp.where(low > high, mixed, 0.0)
    first_diag = jnp.where(eye, mixed + extra[2:3] + base, 0.0)
    last_diag = jnp.where(eye, extra[0:1] + extra[1:2] + base, 0.0)
    first = upper + upper.T + first_diag
    last = lower + lower.T + last_diag
    gram = jnp.concatenate(
        [jnp.concatenate([first, cross], 1), jnp.concatenate([cross.T, last], 1)], 0
    )
    rhs = jnp.concatenate([extra[3:4] + extra[5:6], extra[4:5] + extra[6:7]], 1)
    total = jnp.sum(jnp.sum(first_diag + last_diag, 1, keepdims=True), 0, keepdims=True)
    identity = (iota((K, K), 0) == iota((K, K), 1)).astype(F32)
    error = gram / total
    root = None
    for step in range(NEWTON_STEPS - 1):
        top, rest = split(error)
        half = (0.5 * error).astype(BF16)
        dot = lambda u: jnp.dot(u, half, preferred_element_type=F32)
        if step == 0:
            root = 1.5 * identity - half.astype(F32)
        else:
            root_top, root_rest = split(root)
            root = 1.5 * root - (dot(root_top) + dot(root_rest))
        error = 1.5 * error - (dot(top) + dot(rest))
        top, rest = split(error)
        error = 1.5 * error - (dot(top) + dot(rest))
    root = 1.5 * root - 0.5 * dot3(split(root), split(error))
    once = jnp.sum(root * rhs, 1, keepdims=True) / total
    mean_weight = jnp.sum(root * once, 0, keepdims=True)
    root = jnp.sqrt((K - 1) / total) * root
    first, last = root[:HALF, :HALF], root[HALF:, HALF:]
    out_ref[:HALF, :] = jnp.where(low < high, first, jnp.where(eye, 0.5 * first, last)).astype(BF16)
    out_ref[HALF:K, :] = root[:HALF, HALF:].astype(BF16)
    weights = [mean_weight[:, :HALF], mean_weight[:, HALF:]]
    tops = [w.astype(BF16).astype(F32) for w in weights]
    last_diag = jnp.sum(jnp.where(eye, 0.5 * last, 0.0), 0, keepdims=True)
    rests = [w - t for w, t in zip(weights, tops)]
    extra = jnp.concatenate([last_diag, *tops, *rests, jnp.zeros((3, HALF), F32)], 0)
    out_ref[K:, :] = extra.astype(BF16)


def node_transform(got):
    return pl.pallas_call(
        newton_kernel,
        out_shape=jax.ShapeDtypeStruct((PACKED, HALF), BF16),
        name="newton",
        compiler_params=pltpu.CompilerParams(vmem_limit_bytes=12 << 20),
    )(got)


def analysis_kernel(slot_ref, share_ref, flip_ref, table_ref, state_ref, out_ref):
    step = pl.program_id(0)
    flip_x, flip_y = flip_ref[0], flip_ref[1]
    low, high = iota((HALF, HALF), 0), iota((HALF, HALF), 1)
    eye = low == high
    for n in range(COLS):
        column = step * COLS + n
        cx, cy = column // CY, column % CY
        shares = [share_ref[q, cx, cy] for q in range(4)]
        total = shares[0] + shares[1] + shares[2] + shares[3]
        scale = 1.0 / jnp.full((1, 1), total, F32)
        blend = None
        for q in range(4):
            slot = slot_ref[q, cx, cy]
            ox, oy = slot // 3, slot % 3
            ox = jnp.where(flip_x == 1, ox, 2 - ox)
            oy = jnp.where(flip_y == 1, oy, 2 - oy)
            term = (shares[q] * scale) * table_ref[oy * 3 + ox].astype(F32)
            blend = term if q == 0 else blend + term
        mixed, cross, extra = blend[:HALF], blend[HALF:K], blend[K:]
        upper = jnp.where(low <= high, mixed, 0.0)
        lower = jnp.where(low > high, mixed, jnp.where(eye, extra[0:1], 0.0))
        first = extra[1:2] + extra[3:4]
        last = extra[2:3] + extra[4:5]
        plain = jnp.concatenate(
            [
                jnp.concatenate([upper, cross], 1).astype(BF16),
                jnp.concatenate([jnp.zeros_like(lower), lower], 1).astype(BF16),
            ],
            0,
        )
        turned = jnp.concatenate(
            [
                jnp.concatenate([upper + first, cross + last], 1).astype(BF16),
                jnp.concatenate([jnp.broadcast_to(first, lower.shape), lower + last], 1).astype(BF16),
            ],
            0,
        )
        state = state_ref[n].astype(F32)
        mean = jnp.mean(state, -1, keepdims=True)
        anomaly = (state - mean).astype(BF16)
        update = jnp.dot(anomaly, plain, preferred_element_type=F32) + lax.dot_general(
            anomaly, turned, (((1,), (1,)), ((), ())), preferred_element_type=F32
        )
        out_ref[n] = (mean + update).astype(BF16)


CX = 2
CY = 8
COLS = 4


def analyse(slots, share, flips, table, state):
    columns, levels, width = state.shape
    block = pl.BlockSpec((COLS, levels, width), lambda f, *_: (f, 0, 0))
    return pl.pallas_call(
        analysis_kernel,
        grid_spec=pltpu.PrefetchScalarGridSpec(
            num_scalar_prefetch=3,
            grid=(columns // COLS,),
            in_specs=[pl.BlockSpec((9, PACKED, HALF), lambda f, *_: (0, 0, 0)), block],
            out_specs=block,
        ),
        out_shape=jax.ShapeDtypeStruct(state.shape, BF16),
        name="analysis",
        compiler_params=pltpu.CompilerParams(vmem_limit_bytes=16 << 20),
    )(slots, share, flips, table, state)


def swap(block, axes, count):
    even = [(i, i ^ 1) for i in range(count)]
    odd = [(i, (((i + 1) ^ 1) - 1) % count) for i in range(count)]
    return lax.ppermute(block, axes, even), lax.ppermute(block, axes, odd)


def shards(members, obs_pert, obs_weight, obs_innov, obs_node, neighbour_slot, interp_weight):
    sent = route(obs_node.reshape(1, OBS), obs_weight, obs_innov, obs_pert[0])
    got = lax.all_to_all(sent, ("x", "zl"), split_axis=0, concat_axis=0, tiled=True)
    grams = partial_grams(got)
    grams = lax.all_to_all(grams, "zh", split_axis=0, concat_axis=0, tiled=True)
    own = node_transform(grams)
    even, odd = swap(own, GX, 64)
    line = jnp.stack([even, own, odd])
    even, odd = swap(line, GY, 8)
    table = jnp.concatenate([even, line, odd])
    flips = jnp.stack([lax.axis_index(GX) % 2, lax.axis_index(GY) % 2]).astype(jnp.int32)
    state = members.reshape(CX * CY, *members.shape[2:])
    return analyse(neighbour_slot, interp_weight, flips, table, state).reshape(members.shape)


def solution(mesh):
    fine = Mesh(mesh.devices.reshape(SHAPE), AXES)
    return jax.shard_map(
        shards,
        mesh=fine,
        in_specs=(
            P(GX, GY, None, None),
            P(GY, GX, None),
            P(GY, GX),
            P(GY, GX),
            P(GY, GX, None),
            P(None, GX, GY),
            P(None, GX, GY),
        ),
        out_specs=P(GX, GY, None, None),
        check_vma=False,
    )
```

```python
import jax
import jax.numpy as jnp
from jax import lax
from jax.experimental import pallas as pl
from jax.experimental.pallas import tpu as pltpu
from jax.sharding import Mesh
from jax.sharding import PartitionSpec as P

NEWTON_STEPS = 8
inflation = 1.1

SHAPE = (4, 8, 2, 4, 2)
AXES = ("x", "zh", "zl", "y", "c")
GX = ("x", "zh", "zl")
GY = ("y", "c")

NODES = 64
HIGH = 8
GROUP = 8
CAP = 48
DESTS = 8
OBS = 2048
K = 256
HALF = 128
ROWS = HIGH * CAP + 16
PACKED = K + 8
WIRE = jnp.bfloat16
F32 = jnp.float32
BF16 = jnp.bfloat16


def iota(shape, dim):
    return lax.broadcasted_iota(jnp.int32, shape, dim)


def route_kernel(
    node_hbm, weight_hbm, innov_hbm, pert_hbm, out_ref,
    rank_ref, scaled_ref, factor_ref, node_ref, weight_ref, innov_ref, pert_ref, sems,
):
    step = pl.program_id(0)

    @pl.when(step == 0)
    def _():
        pairs = (
            (node_hbm, node_ref), (pert_hbm, pert_ref), (weight_hbm, weight_ref), (innov_hbm, innov_ref),
        )
        copies = [pltpu.make_async_copy(a, b, sems.at[i]) for i, (a, b) in enumerate(pairs)]
        for copy in copies:
            copy.start()
        copies[0].wait()
        row = iota((NODES, 1), 0)
        name = (row // 16) * 16 + (row % 8) * 2 + (row // 8) % 2
        onehot = (node_ref[...] == name).astype(F32)
        upper = (iota((K, K), 0) <= iota((K, K), 1)).astype(BF16)
        blocks = [onehot[:, b * K : (b + 1) * K] for b in range(OBS // K)]
        counts = jnp.dot(
            jnp.concatenate(blocks, 0).astype(BF16), upper, preferred_element_type=F32
        )
        carry = jnp.zeros((NODES, 1), F32)
        for b, block in enumerate(blocks):
            count = counts[b * NODES : (b + 1) * NODES]
            rank_ref[:, b * K : (b + 1) * K] = jnp.where(block > 0, count + (carry - 1.0), -1.0)
            carry += count[:, K - 1 : K]
        for copy in copies[1:]:
            copy.wait()
        side = jnp.sqrt(weight_ref[...].astype(F32))
        factor = onehot * (side * innov_ref[...].astype(F32))
        top = factor.astype(BF16)
        factor_ref[:NODES, :] = top
        factor_ref[NODES:, :] = (factor - top.astype(F32)).astype(BF16)
        side = jnp.concatenate([side[:, k * 128 : (k + 1) * 128] for k in range(OBS // 128)], 0).T
        for k in range(OBS // 128):
            rows = pl.ds(k * 128, 128)
            scaled_ref[rows, :] = (pert_ref[rows, :].astype(F32) * side[:, k : k + 1]).astype(BF16)

    rows = pl.ds(pl.multiple_of(step * DESTS * HIGH, DESTS * HIGH), DESTS * HIGH)
    more = pl.ds(pl.multiple_of(NODES + step * DESTS * HIGH, DESTS * HIGH), DESTS * HIGH)
    rank = rank_ref[rows, :]
    wanted = iota((CAP, OBS), 0).astype(F32)
    pick = jnp.concatenate(
        [(rank[h : h + 1, :] == wanted).astype(BF16) for h in range(DESTS * HIGH)]
        + [factor_ref[rows, :], factor_ref[more, :]],
        0,
    )
    picked = jnp.dot(pick, scaled_ref[...], preferred_element_type=F32)
    count = DESTS * HIGH
    rhs = picked[count * CAP : count * CAP + count] + picked[count * CAP + count :]
    picked = picked[: count * CAP].astype(BF16)
    top = rhs.astype(BF16).astype(F32)
    rest = rhs - top
    for d in range(DESTS):
        out_ref[d, : HIGH * CAP, :] = picked[d * HIGH * CAP : (d + 1) * HIGH * CAP]
        mine = slice(d * HIGH, (d + 1) * HIGH)
        out_ref[d, HIGH * CAP :, :] = jnp.concatenate([top[mine], rest[mine]], 0).astype(BF16)


def route(node, weight, innov, pert):
    return pl.pallas_call(
        route_kernel,
        grid=(GROUP // DESTS,),
        in_specs=[pl.BlockSpec(memory_space=pltpu.HBM)] * 4,
        out_specs=pl.BlockSpec((DESTS, ROWS, K), lambda d: (d, 0, 0)),
        out_shape=jax.ShapeDtypeStruct((GROUP, ROWS, K), BF16),
        scratch_shapes=[
            pltpu.VMEM((NODES, OBS), F32),
            pltpu.VMEM((OBS, K), BF16),
            pltpu.VMEM((2 * NODES, OBS), BF16),
            pltpu.VMEM((1, OBS), jnp.int32),
            pltpu.VMEM((1, OBS), BF16),
            pltpu.VMEM((1, OBS), BF16),
            pltpu.VMEM((OBS, K), BF16),
            pltpu.SemaphoreType.DMA((4,)),
        ],
        name="route",
        compiler_params=pltpu.CompilerParams(vmem_limit_bytes=40 << 20),
    )(*[pltpu.with_memory_space_constraint(v, pltpu.HBM) for v in (node, weight, innov, pert)])


PER = 2


def gram_kernel(obs_ref, side_ref, out_ref):
    step = pl.program_id(0)
    low, high = iota((HALF, HALF), 0), iota((HALF, HALF), 1)
    eye = low == high
    keep = low <= high
    rest = lambda v: v - v.astype(WIRE).astype(F32)
    sides = jnp.sum(side_ref[...].astype(F32), 0)
    name = iota((16, K), 0) % HIGH
    for n in range(PER):
        obs = obs_ref[:, n * CAP : (n + 1) * CAP, :].reshape(GROUP * CAP, K)
        gram = lax.dot_general(obs, obs, (((0,), (0,)), ((), ())), preferred_element_type=F32)
        first, cross, last = gram[:HALF, :HALF], gram[:HALF, HALF:], gram[HALF:, HALF:]
        first_diag = jnp.sum(jnp.where(eye, first, 0.0), 0, keepdims=True)
        last_diag = jnp.sum(jnp.where(eye, last, 0.0), 0, keepdims=True)
        rhs = jnp.sum(jnp.where(name == step * PER + n, sides, 0.0), 0, keepdims=True)
        out_ref[n, :HALF, :] = jnp.where(keep, first, last).astype(WIRE)
        out_ref[n, HALF:K, :] = cross.astype(WIRE)
        extra = jnp.concatenate(
            [
                last_diag,
                rest(last_diag),
                rest(first_diag),
                rhs[:, :HALF],
                rhs[:, HALF:],
                rest(rhs[:, :HALF]),
                rest(rhs[:, HALF:]),
                jnp.zeros((1, HALF), F32),
            ],
            0,
        )
        out_ref[n, K:, :] = extra.astype(WIRE)


def partial_grams(got):
    return pl.pallas_call(
        gram_kernel,
        grid=(HIGH // PER,),
        in_specs=[
            pl.BlockSpec((GROUP, PER * CAP, K), lambda h: (0, h, 0)),
            pl.BlockSpec((GROUP, 16, K), lambda h: (0, HIGH * CAP // 16, 0)),
        ],
        out_specs=pl.BlockSpec((PER, PACKED, HALF), lambda h: (h, 0, 0)),
        out_shape=jax.ShapeDtypeStruct((HIGH, PACKED, HALF), WIRE),
        name="gram",
        compiler_params=pltpu.CompilerParams(vmem_limit_bytes=16 << 20),
    )(got, got)


def split(a):
    top = a.astype(BF16)
    return top, (a - top.astype(F32)).astype(BF16)


def dot3(a, b):
    (a_top, a_rest), (b_top, b_rest) = a, b
    dot = lambda u, v: jnp.dot(u, v, preferred_element_type=F32)
    return dot(a_top, b_top) + (dot(a_top, b_rest) + dot(a_rest, b_top))


def newton_kernel(got_ref, out_ref):
    packed = jnp.sum(got_ref[...].astype(F32), 0)
    mixed, cross, extra = packed[:HALF], packed[HALF:K], packed[K:]
    low, high = iota((HALF, HALF), 0), iota((HALF, HALF), 1)
    eye = low == high
    base = (K - 1) / inflation
    upper = jnp.where(low < high, mixed, 0.0)
    lower = jnp.where(low > high, mixed, 0.0)
    first_diag = jnp.where(eye, mixed + extra[2:3] + base, 0.0)
    last_diag = jnp.where(eye, extra[0:1] + extra[1:2] + base, 0.0)
    first = upper + upper.T + first_diag
    last = lower + lower.T + last_diag
    gram = jnp.concatenate(
        [jnp.concatenate([first, cross], 1), jnp.concatenate([cross.T, last], 1)], 0
    )
    rhs = jnp.concatenate([extra[3:4] + extra[5:6], extra[4:5] + extra[6:7]], 1)
    total = jnp.sum(jnp.sum(first_diag + last_diag, 1, keepdims=True), 0, keepdims=True)
    identity = (iota((K, K), 0) == iota((K, K), 1)).astype(F32)
    error = gram / total
    root = None
    for step in range(NEWTON_STEPS - 1):
        half = (0.5 * error).astype(BF16)

        def times(*values):
            parts = [p for v in values for p in split(v)]
            out = jnp.dot(jnp.concatenate(parts, 0), half, preferred_element_type=F32)
            return [
                1.5 * v - (out[2 * i * K : (2 * i + 1) * K] + out[(2 * i + 1) * K : (2 * i + 2) * K])
                for i, v in enumerate(values)
            ]

        if step == 0:
            root = 1.5 * identity - half.astype(F32)
            (error,) = times(error)
        else:
            error, root = times(error, root)
        (error,) = times(error)
    root = 1.5 * root - 0.5 * dot3(split(root), split(error))
    once = jnp.sum(root * rhs, 1, keepdims=True) / total
    mean_weight = jnp.sum(root * once, 0, keepdims=True)
    root = jnp.sqrt((K - 1) / total) * root
    first, last = root[:HALF, :HALF], root[HALF:, HALF:]
    out_ref[:HALF, :] = jnp.where(low < high, first, jnp.where(eye, 0.5 * first, last)).astype(BF16)
    out_ref[HALF:K, :] = root[:HALF, HALF:].astype(BF16)
    weights = [mean_weight[:, :HALF], mean_weight[:, HALF:]]
    tops = [w.astype(BF16).astype(F32) for w in weights]
    last_diag = jnp.sum(jnp.where(eye, 0.5 * last, 0.0), 0, keepdims=True)
    rests = [w - t for w, t in zip(weights, tops)]
    extra = jnp.concatenate([last_diag, *tops, *rests, jnp.zeros((3, HALF), F32)], 0)
    out_ref[K:, :] = extra.astype(BF16)


def node_transform(got):
    return pl.pallas_call(
        newton_kernel,
        out_shape=jax.ShapeDtypeStruct((PACKED, HALF), BF16),
        name="newton",
        compiler_params=pltpu.CompilerParams(vmem_limit_bytes=12 << 20),
    )(got)


def analysis_kernel(slot_ref, share_ref, flip_ref, table_ref, state_ref, out_ref):
    step = pl.program_id(0)
    flip_x, flip_y = flip_ref[0], flip_ref[1]
    low, high = iota((HALF, HALF), 0), iota((HALF, HALF), 1)
    eye = low == high
    for n in range(COLS):
        column = step * COLS + n
        cx, cy = column // CY, column % CY
        shares = [share_ref[q, cx, cy] for q in range(4)]
        total = shares[0] + shares[1] + shares[2] + shares[3]
        scale = 1.0 / jnp.full((1, 1), total, F32)
        blend = None
        for q in range(4):
            slot = slot_ref[q, cx, cy]
            ox, oy = slot // 3, slot % 3
            ox = jnp.where(flip_x == 1, ox, 2 - ox)
            oy = jnp.where(flip_y == 1, oy, 2 - oy)
            term = (shares[q] * scale) * table_ref[oy * 3 + ox].astype(F32)
            blend = term if q == 0 else blend + term
        mixed, cross, extra = blend[:HALF], blend[HALF:K], blend[K:]
        upper = jnp.where(low <= high, mixed, 0.0)
        lower = jnp.where(low > high, mixed, jnp.where(eye, extra[0:1], 0.0))
        first = extra[1:2] + extra[3:4]
        last = extra[2:3] + extra[4:5]
        plain = jnp.concatenate(
            [
                jnp.concatenate([upper, cross], 1).astype(BF16),
                jnp.concatenate([jnp.zeros_like(lower), lower], 1).astype(BF16),
            ],
            0,
        )
        turned = jnp.concatenate(
            [
                jnp.concatenate([upper + first, cross + last], 1).astype(BF16),
                jnp.concatenate([jnp.broadcast_to(first, lower.shape), lower + last], 1).astype(BF16),
            ],
            0,
        )
        state = state_ref[n].astype(F32)
        mean = jnp.mean(state, -1, keepdims=True)
        anomaly = (state - mean).astype(BF16)
        update = jnp.dot(anomaly, plain, preferred_element_type=F32) + lax.dot_general(
            anomaly, turned, (((1,), (1,)), ((), ())), preferred_element_type=F32
        )
        out_ref[n] = (mean + update).astype(BF16)


CX = 2
CY = 8
COLS = 16


def analyse(slots, share, flips, table, state):
    columns, levels, width = state.shape
    block = pl.BlockSpec((COLS, levels, width), lambda f, *_: (f, 0, 0))
    return pl.pallas_call(
        analysis_kernel,
        grid_spec=pltpu.PrefetchScalarGridSpec(
            num_scalar_prefetch=3,
            grid=(columns // COLS,),
            in_specs=[pl.BlockSpec((9, PACKED, HALF), lambda f, *_: (0, 0, 0)), block],
            out_specs=block,
        ),
        out_shape=jax.ShapeDtypeStruct(state.shape, BF16),
        name="analysis",
        compiler_params=pltpu.CompilerParams(vmem_limit_bytes=16 << 20),
    )(slots, share, flips, table, state)


def swap(block, axes, count):
    even = [(i, i ^ 1) for i in range(count)]
    odd = [(i, (((i + 1) ^ 1) - 1) % count) for i in range(count)]
    return lax.ppermute(block, axes, even), lax.ppermute(block, axes, odd)


def shards(members, obs_pert, obs_weight, obs_innov, obs_node, neighbour_slot, interp_weight):
    sent = route(obs_node.reshape(1, OBS), obs_weight, obs_innov, obs_pert[0])
    got = lax.all_to_all(sent, ("x", "zl"), split_axis=0, concat_axis=0, tiled=True)
    grams = partial_grams(got)
    grams = lax.all_to_all(grams, "zh", split_axis=0, concat_axis=0, tiled=True)
    own = node_transform(grams)
    even, odd = swap(own, GX, 64)
    line = jnp.stack([even, own, odd])
    even, odd = swap(line, GY, 8)
    table = jnp.concatenate([even, line, odd])
    flips = jnp.stack([lax.axis_index(GX) % 2, lax.axis_index(GY) % 2]).astype(jnp.int32)
    state = members.reshape(CX * CY, *members.shape[2:])
    return analyse(neighbour_slot, interp_weight, flips, table, state).reshape(members.shape)


def solution(mesh):
    fine = Mesh(mesh.devices.reshape(SHAPE), AXES)
    return jax.shard_map(
        shards,
        mesh=fine,
        in_specs=(
            P(GX, GY, None, None),
            P(GY, GX, None),
            P(GY, GX),
            P(GY, GX),
            P(GY, GX, None),
            P(None, GX, GY),
            P(None, GX, GY),
        ),
        out_specs=P(GX, GY, None, None),
        check_vma=False,
    )
```

```python
import jax
import jax.numpy as jnp
from jax import lax
from jax.experimental import pallas as pl
from jax.experimental.pallas import tpu as pltpu
from jax.sharding import Mesh
from jax.sharding import PartitionSpec as P


NEWTON_STEPS = 8
inflation = 1.1

SHAPE = (4, 8, 2, 4, 2)
AXES = ("x", "zh", "zl", "y", "c")
GX = ("x", "zh", "zl")
GY = ("y", "c")

NODES = 64
HIGH = 8
GROUP = 8
CAP = 48
DESTS = 8
OBS = 2048
K = 256
HALF = 128
ROWS = HIGH * CAP + 16
PACKED = K + 8
WIRE = jnp.bfloat16
F32 = jnp.float32
BF16 = jnp.bfloat16


def iota(shape, dim):
    return lax.broadcasted_iota(jnp.int32, shape, dim)


def route_kernel(
    node_hbm, weight_hbm, innov_hbm, pert_hbm, out_ref,
    rank_ref, scaled_ref, factor_ref, node_ref, weight_ref, innov_ref, pert_ref, sems,
):
    step = pl.program_id(0)

    @pl.when(step == 0)
    def _():
        pairs = (
            (node_hbm, node_ref), (pert_hbm, pert_ref), (weight_hbm, weight_ref), (innov_hbm, innov_ref),
        )
        copies = [pltpu.make_async_copy(a, b, sems.at[i]) for i, (a, b) in enumerate(pairs)]
        for copy in copies:
            copy.start()
        copies[0].wait()
        row = iota((NODES, 1), 0)
        name = (row // 16) * 16 + (row % 8) * 2 + (row // 8) % 2
        onehot = (node_ref[...] == name).astype(F32)
        upper = (iota((K, K), 0) <= iota((K, K), 1)).astype(BF16)
        blocks = [onehot[:, b * K : (b + 1) * K] for b in range(OBS // K)]
        counts = jnp.dot(
            jnp.concatenate(blocks, 0).astype(BF16), upper, preferred_element_type=F32
        )
        carry = jnp.zeros((NODES, 1), F32)
        for b, block in enumerate(blocks):
            count = counts[b * NODES : (b + 1) * NODES]
            rank_ref[:, b * K : (b + 1) * K] = jnp.where(block > 0, count + (carry - 1.0), -1.0)
            carry += count[:, K - 1 : K]
        for copy in copies[1:]:
            copy.wait()
        side = jnp.sqrt(weight_ref[...].astype(F32))
        factor = onehot * (side * innov_ref[...].astype(F32))
        top = factor.astype(BF16)
        factor_ref[:NODES, :] = top
        factor_ref[NODES:, :] = (factor - top.astype(F32)).astype(BF16)
        side = jnp.concatenate([side[:, k * 128 : (k + 1) * 128] for k in range(OBS // 128)], 0).T
        for k in range(OBS // 128):
            rows = pl.ds(k * 128, 128)
            scaled_ref[rows, :] = (pert_ref[rows, :].astype(F32) * side[:, k : k + 1]).astype(BF16)

    rows = pl.ds(pl.multiple_of(step * DESTS * HIGH, DESTS * HIGH), DESTS * HIGH)
    more = pl.ds(pl.multiple_of(NODES + step * DESTS * HIGH, DESTS * HIGH), DESTS * HIGH)
    rank = rank_ref[rows, :]
    wanted = iota((CAP, OBS), 0).astype(F32)
    pick = jnp.concatenate(
        [(rank[h : h + 1, :] == wanted).astype(BF16) for h in range(DESTS * HIGH)]
        + [factor_ref[rows, :], factor_ref[more, :]],
        0,
    )
    picked = jnp.dot(pick, scaled_ref[...], preferred_element_type=F32)
    count = DESTS * HIGH
    rhs = picked[count * CAP : count * CAP + count] + picked[count * CAP + count :]
    picked = picked[: count * CAP].astype(BF16)
    top = rhs.astype(BF16).astype(F32)
    rest = rhs - top
    for d in range(DESTS):
        out_ref[d, : HIGH * CAP, :] = picked[d * HIGH * CAP : (d + 1) * HIGH * CAP]
        mine = slice(d * HIGH, (d + 1) * HIGH)
        out_ref[d, HIGH * CAP :, :] = jnp.concatenate([top[mine], rest[mine]], 0).astype(BF16)


def route(node, weight, innov, pert):
    return pl.pallas_call(
        route_kernel,
        grid=(GROUP // DESTS,),
        in_specs=[pl.BlockSpec(memory_space=pltpu.HBM)] * 4,
        out_specs=pl.BlockSpec((DESTS, ROWS, K), lambda d: (d, 0, 0)),
        out_shape=jax.ShapeDtypeStruct((GROUP, ROWS, K), BF16),
        scratch_shapes=[
            pltpu.VMEM((NODES, OBS), F32),
            pltpu.VMEM((OBS, K), BF16),
            pltpu.VMEM((2 * NODES, OBS), BF16),
            pltpu.VMEM((1, OBS), jnp.int32),
            pltpu.VMEM((1, OBS), BF16),
            pltpu.VMEM((1, OBS), BF16),
            pltpu.VMEM((OBS, K), BF16),
            pltpu.SemaphoreType.DMA((4,)),
        ],
        name="route",
        compiler_params=pltpu.CompilerParams(vmem_limit_bytes=40 << 20),
    )(*[pltpu.with_memory_space_constraint(v, pltpu.HBM) for v in (node, weight, innov, pert)])


PER = 2


def gram_kernel(obs_ref, side_ref, out_ref):
    step = pl.program_id(0)
    low, high = iota((HALF, HALF), 0), iota((HALF, HALF), 1)
    eye = low == high
    keep = low <= high
    rest = lambda v: v - v.astype(WIRE).astype(F32)
    sides = jnp.sum(side_ref[...].astype(F32), 0)
    name = iota((16, K), 0) % HIGH
    for n in range(PER):
        obs = obs_ref[:, n * CAP : (n + 1) * CAP, :].reshape(GROUP * CAP, K)
        gram = lax.dot_general(obs, obs, (((0,), (0,)), ((), ())), preferred_element_type=F32)
        first, cross, last = gram[:HALF, :HALF], gram[:HALF, HALF:], gram[HALF:, HALF:]
        first_diag = jnp.sum(jnp.where(eye, first, 0.0), 0, keepdims=True)
        last_diag = jnp.sum(jnp.where(eye, last, 0.0), 0, keepdims=True)
        rhs = jnp.sum(jnp.where(name == step * PER + n, sides, 0.0), 0, keepdims=True)
        out_ref[n, :HALF, :] = jnp.where(keep, first, last).astype(WIRE)
        out_ref[n, HALF:K, :] = cross.astype(WIRE)
        extra = jnp.concatenate(
            [
                last_diag,
                rest(last_diag),
                rest(first_diag),
                rhs[:, :HALF],
                rhs[:, HALF:],
                rest(rhs[:, :HALF]),
                rest(rhs[:, HALF:]),
                jnp.zeros((1, HALF), F32),
            ],
            0,
        )
        out_ref[n, K:, :] = extra.astype(WIRE)


def partial_grams(got):
    return pl.pallas_call(
        gram_kernel,
        grid=(HIGH // PER,),
        in_specs=[
            pl.BlockSpec((GROUP, PER * CAP, K), lambda h: (0, h, 0)),
            pl.BlockSpec((GROUP, 16, K), lambda h: (0, HIGH * CAP // 16, 0)),
        ],
        out_specs=pl.BlockSpec((PER, PACKED, HALF), lambda h: (h, 0, 0)),
        out_shape=jax.ShapeDtypeStruct((HIGH, PACKED, HALF), WIRE),
        name="gram",
        compiler_params=pltpu.CompilerParams(vmem_limit_bytes=16 << 20),
    )(got, got)


def split(a):
    top = a.astype(BF16)
    return top, (a - top.astype(F32)).astype(BF16)


def dot3(a, b):
    (a_top, a_rest), (b_top, b_rest) = a, b
    dot = lambda u, v: jnp.dot(u, v, preferred_element_type=F32)
    return dot(a_top, b_top) + (dot(a_top, b_rest) + dot(a_rest, b_top))


def newton_kernel(got_ref, out_ref):
    packed = jnp.sum(got_ref[...].astype(F32), 0)
    mixed, cross, extra = packed[:HALF], packed[HALF:K], packed[K:]
    low, high = iota((HALF, HALF), 0), iota((HALF, HALF), 1)
    eye = low == high
    base = (K - 1) / inflation
    upper = jnp.where(low < high, mixed, 0.0)
    lower = jnp.where(low > high, mixed, 0.0)
    first_diag = jnp.where(eye, mixed + extra[2:3] + base, 0.0)
    last_diag = jnp.where(eye, extra[0:1] + extra[1:2] + base, 0.0)
    first = upper + upper.T + first_diag
    last = lower + lower.T + last_diag
    gram = jnp.concatenate(
        [jnp.concatenate([first, cross], 1), jnp.concatenate([cross.T, last], 1)], 0
    )
    rhs = jnp.concatenate([extra[3:4] + extra[5:6], extra[4:5] + extra[6:7]], 1)
    total = jnp.sum(jnp.sum(first_diag + last_diag, 1, keepdims=True), 0, keepdims=True)
    identity = (iota((K, K), 0) == iota((K, K), 1)).astype(F32)
    error = gram / total
    root = None
    for step in range(NEWTON_STEPS - 1):
        half = (0.5 * error).astype(BF16)

        def times(*values):
            parts = [p for v in values for p in split(v)]
            out = jnp.dot(jnp.concatenate(parts, 0), half, preferred_element_type=F32)
            return [
                1.5 * v - (out[2 * i * K : (2 * i + 1) * K] + out[(2 * i + 1) * K : (2 * i + 2) * K])
                for i, v in enumerate(values)
            ]

        if step == 0:
            root = 1.5 * identity - half.astype(F32)
            (error,) = times(error)
        else:
            error, root = times(error, root)
        (error,) = times(error)
    root = 1.5 * root - 0.5 * dot3(split(root), split(error))
    once = jnp.sum(root * rhs, 1, keepdims=True) / total
    mean_weight = jnp.sum(root * once, 0, keepdims=True)
    root = jnp.sqrt((K - 1) / total) * root
    first, last = root[:HALF, :HALF], root[HALF:, HALF:]
    out_ref[:HALF, :] = jnp.where(low < high, first, jnp.where(eye, 0.5 * first, last)).astype(BF16)
    out_ref[HALF:K, :] = root[:HALF, HALF:].astype(BF16)
    weights = [mean_weight[:, :HALF], mean_weight[:, HALF:]]
    tops = [w.astype(BF16).astype(F32) for w in weights]
    last_diag = jnp.sum(jnp.where(eye, 0.5 * last, 0.0), 0, keepdims=True)
    rests = [w - t for w, t in zip(weights, tops)]
    extra = jnp.concatenate([last_diag, *tops, *rests, jnp.zeros((3, HALF), F32)], 0)
    out_ref[K:, :] = extra.astype(BF16)


def node_transform(got):
    return pl.pallas_call(
        newton_kernel,
        out_shape=jax.ShapeDtypeStruct((PACKED, HALF), BF16),
        name="newton",
        compiler_params=pltpu.CompilerParams(vmem_limit_bytes=12 << 20),
    )(got)


def analysis_kernel(slot_ref, share_ref, flip_ref, table_ref, state_ref, out_hbm, out_ref, sems):
    copies = []
    flip_x, flip_y = flip_ref[0], flip_ref[1]
    low, high = iota((HALF, HALF), 0), iota((HALF, HALF), 1)
    eye = low == high
    for n in range(COLS):
        cx, cy = n // CY, n % CY
        shares = [share_ref[q, cx, cy] for q in range(4)]
        total = shares[0] + shares[1] + shares[2] + shares[3]
        scale = 1.0 / jnp.full((1, 1), total, F32)
        blend = None
        for q in range(4):
            slot = slot_ref[q, cx, cy]
            ox, oy = slot // 3, slot % 3
            ox = jnp.where(flip_x == 1, ox, 2 - ox)
            oy = jnp.where(flip_y == 1, oy, 2 - oy)
            term = (shares[q] * scale) * table_ref[oy * 3 + ox].astype(F32)
            blend = term if q == 0 else blend + term
        mixed, cross, extra = blend[:HALF], blend[HALF:K], blend[K:]
        upper = jnp.where(low <= high, mixed, 0.0)
        lower = jnp.where(low > high, mixed, jnp.where(eye, extra[0:1], 0.0))
        first = extra[1:2] + extra[3:4]
        last = extra[2:3] + extra[4:5]
        plain = jnp.concatenate(
            [
                jnp.concatenate([upper, cross], 1).astype(BF16),
                jnp.concatenate([jnp.zeros_like(lower), lower], 1).astype(BF16),
            ],
            0,
        )
        turned = jnp.concatenate(
            [
                jnp.concatenate([upper + first, cross + last], 1).astype(BF16),
                jnp.concatenate([jnp.broadcast_to(first, lower.shape), lower + last], 1).astype(BF16),
            ],
            0,
        )
        state = state_ref[n].astype(F32)
        mean = jnp.mean(state, -1, keepdims=True)
        anomaly = (state - mean).astype(BF16)
        update = jnp.dot(anomaly, plain, preferred_element_type=F32) + lax.dot_general(
            anomaly, turned, (((1,), (1,)), ((), ())), preferred_element_type=F32
        )
        out_ref[n] = (mean + update).astype(BF16)
        copies.append(pltpu.make_async_copy(out_ref.at[n], out_hbm.at[n], sems.at[n]))
        copies[-1].start()
    for copy in copies:
        copy.wait()


CX = 2
CY = 8
COLS = 16


def analyse(slots, share, flips, table, state):
    columns, levels, width = state.shape
    block = pl.BlockSpec((COLS, levels, width), lambda f, *_: (f, 0, 0))
    return pl.pallas_call(
        analysis_kernel,
        grid_spec=pltpu.PrefetchScalarGridSpec(
            num_scalar_prefetch=3,
            grid=(columns // COLS,),
            in_specs=[pl.BlockSpec((9, PACKED, HALF), lambda f, *_: (0, 0, 0)), block],
            out_specs=pl.BlockSpec(memory_space=pltpu.HBM),
            scratch_shapes=[pltpu.VMEM((COLS, levels, width), BF16), pltpu.SemaphoreType.DMA((COLS,))],
        ),
        out_shape=jax.ShapeDtypeStruct(state.shape, BF16),
        name="analysis",
        compiler_params=pltpu.CompilerParams(vmem_limit_bytes=16 << 20),
    )(slots, share, flips, table, state)


def swap(block, axes, count):
    even = [(i, i ^ 1) for i in range(count)]
    odd = [(i, (((i + 1) ^ 1) - 1) % count) for i in range(count)]
    far = lax.ppermute(block, axes, odd)
    near = lax.ppermute(block, axes, even)
    return near, far


def shards(members, obs_pert, obs_weight, obs_innov, obs_node, neighbour_slot, interp_weight):
    sent = route(obs_node.reshape(1, OBS), obs_weight, obs_innov, obs_pert[0])
    got = lax.all_to_all(sent, ("x", "zl"), split_axis=0, concat_axis=0, tiled=True)
    grams = partial_grams(got)
    grams = lax.all_to_all(grams, "zh", split_axis=0, concat_axis=0, tiled=True)
    own = node_transform(grams)
    even, odd = swap(own, GX, 64)
    line = jnp.stack([even, own, odd])
    even, odd = swap(line, GY, 8)
    table = jnp.concatenate([even, line, odd])
    flips = jnp.stack([lax.axis_index(GX) % 2, lax.axis_index(GY) % 2]).astype(jnp.int32)
    state = members.reshape(CX * CY, *members.shape[2:])
    return analyse(neighbour_slot, interp_weight, flips, table, state).reshape(members.shape)


def solution(mesh):
    fine = Mesh(mesh.devices.reshape(SHAPE), AXES)
    return jax.shard_map(
        shards,
        mesh=fine,
        in_specs=(
            P(GX, GY, None, None),
            P(GY, GX, None),
            P(GY, GX),
            P(GY, GX),
            P(GY, GX, None),
            P(None, GX, GY),
            P(None, GX, GY),
        ),
        out_specs=P(GX, GY, None, None),
        check_vma=False,
    )
```

```python
import jax
import jax.numpy as jnp
from jax import lax
from jax.experimental import pallas as pl
from jax.experimental.pallas import tpu as pltpu
from jax.sharding import Mesh
from jax.sharding import PartitionSpec as P


NEWTON_STEPS = 8
COARSE_STEPS = 4
inflation = 1.1

SHAPE = (4, 8, 2, 4, 2)
AXES = ("x", "zh", "zl", "y", "c")
GX = ("x", "zh", "zl")
GY = ("y", "c")

NODES = 64
HIGH = 8
GROUP = 8
CAP = 48
DESTS = 8
OBS = 2048
K = 256
HALF = 128
ROWS = HIGH * CAP + 16
PACKED = K + 8
WIRE = jnp.int16
STEPS_16 = 32767.0
F32 = jnp.float32
BF16 = jnp.bfloat16


def iota(shape, dim):
    return lax.broadcasted_iota(jnp.int32, shape, dim)


def route_kernel(
    node_hbm, weight_hbm, innov_hbm, pert_hbm, out_ref,
    rank_ref, scaled_ref, factor_ref, node_ref, weight_ref, innov_ref, pert_ref, sems,
):
    step = pl.program_id(0)

    @pl.when(step == 0)
    def _():
        pairs = (
            (node_hbm, node_ref), (pert_hbm, pert_ref), (weight_hbm, weight_ref), (innov_hbm, innov_ref),
        )
        copies = [pltpu.make_async_copy(a, b, sems.at[i]) for i, (a, b) in enumerate(pairs)]
        for copy in copies:
            copy.start()
        copies[0].wait()
        row = iota((NODES, 1), 0)
        name = (row // 16) * 16 + (row % 8) * 2 + (row // 8) % 2
        onehot = (node_ref[...] == name).astype(F32)
        upper = (iota((K, K), 0) <= iota((K, K), 1)).astype(BF16)
        blocks = [onehot[:, b * K : (b + 1) * K] for b in range(OBS // K)]
        counts = jnp.dot(
            jnp.concatenate(blocks, 0).astype(BF16), upper, preferred_element_type=F32
        )
        carry = jnp.zeros((NODES, 1), F32)
        for b, block in enumerate(blocks):
            count = counts[b * NODES : (b + 1) * NODES]
            rank_ref[:, b * K : (b + 1) * K] = jnp.where(block > 0, count + (carry - 1.0), -1.0)
            carry += count[:, K - 1 : K]
        for copy in copies[1:]:
            copy.wait()
        side = jnp.sqrt(weight_ref[...].astype(F32))
        factor = onehot * (side * innov_ref[...].astype(F32))
        top = factor.astype(BF16)
        factor_ref[:NODES, :] = top
        factor_ref[NODES:, :] = (factor - top.astype(F32)).astype(BF16)
        side = jnp.concatenate([side[:, k * 128 : (k + 1) * 128] for k in range(OBS // 128)], 0).T
        for k in range(OBS // 128):
            rows = pl.ds(k * 128, 128)
            scaled_ref[rows, :] = (pert_ref[rows, :].astype(F32) * side[:, k : k + 1]).astype(BF16)

    rows = pl.ds(pl.multiple_of(step * DESTS * HIGH, DESTS * HIGH), DESTS * HIGH)
    more = pl.ds(pl.multiple_of(NODES + step * DESTS * HIGH, DESTS * HIGH), DESTS * HIGH)
    rank = rank_ref[rows, :]
    wanted = iota((CAP, OBS), 0).astype(F32)
    pick = jnp.concatenate(
        [(rank[h : h + 1, :] == wanted).astype(BF16) for h in range(DESTS * HIGH)]
        + [factor_ref[rows, :], factor_ref[more, :]],
        0,
    )
    picked = jnp.dot(pick, scaled_ref[...], preferred_element_type=F32)
    count = DESTS * HIGH
    rhs = picked[count * CAP : count * CAP + count] + picked[count * CAP + count :]
    picked = picked[: count * CAP].astype(BF16)
    top = rhs.astype(BF16).astype(F32)
    rest = rhs - top
    for d in range(DESTS):
        out_ref[d, : HIGH * CAP, :] = picked[d * HIGH * CAP : (d + 1) * HIGH * CAP]
        mine = slice(d * HIGH, (d + 1) * HIGH)
        out_ref[d, HIGH * CAP :, :] = jnp.concatenate([top[mine], rest[mine]], 0).astype(BF16)


def route(node, weight, innov, pert):
    return pl.pallas_call(
        route_kernel,
        grid=(GROUP // DESTS,),
        in_specs=[pl.BlockSpec(memory_space=pltpu.HBM)] * 4,
        out_specs=pl.BlockSpec((DESTS, ROWS, K), lambda d: (d, 0, 0)),
        out_shape=jax.ShapeDtypeStruct((GROUP, ROWS, K), BF16),
        scratch_shapes=[
            pltpu.VMEM((NODES, OBS), F32),
            pltpu.VMEM((OBS, K), BF16),
            pltpu.VMEM((2 * NODES, OBS), BF16),
            pltpu.VMEM((1, OBS), jnp.int32),
            pltpu.VMEM((1, OBS), BF16),
            pltpu.VMEM((1, OBS), BF16),
            pltpu.VMEM((OBS, K), BF16),
            pltpu.SemaphoreType.DMA((4,)),
        ],
        name="route",
        compiler_params=pltpu.CompilerParams(vmem_limit_bytes=40 << 20),
    )(*[pltpu.with_memory_space_constraint(v, pltpu.HBM) for v in (node, weight, innov, pert)])


PER = 2


def code(value, bound):
    scaled = jnp.floor(value * (STEPS_16 / bound) + 0.5)
    return scaled.astype(jnp.int32).astype(WIRE)


def bound_of(value):
    most = jnp.max(jnp.max(jnp.abs(value), 1, keepdims=True), 0, keepdims=True)
    return jnp.floor(most) + 1.0


def gram_kernel(obs_ref, side_ref, out_ref):
    step = pl.program_id(0)
    low, high = iota((HALF, HALF), 0), iota((HALF, HALF), 1)
    eye = low == high
    keep = low <= high
    sides = jnp.sum(side_ref[...].astype(F32), 0)
    name = iota((16, K), 0) % HIGH
    for n in range(PER):
        obs = obs_ref[:, n * CAP : (n + 1) * CAP, :].reshape(GROUP * CAP, K)
        gram = lax.dot_general(obs, obs, (((0,), (0,)), ((), ())), preferred_element_type=F32)
        first, cross, last = gram[:HALF, :HALF], gram[:HALF, HALF:], gram[HALF:, HALF:]
        first_diag = jnp.sum(jnp.where(eye, first, 0.0), 0, keepdims=True)
        last_diag = jnp.sum(jnp.where(eye, last, 0.0), 0, keepdims=True)
        rhs = jnp.sum(jnp.where(name == step * PER + n, sides, 0.0), 0, keepdims=True)
        bound = bound_of(jnp.maximum(first_diag, last_diag))
        rhs_bound = bound_of(rhs)
        out_ref[n, :HALF, :] = code(jnp.where(keep, first, last), bound)
        out_ref[n, HALF:K, :] = code(cross, bound)
        extra = jnp.concatenate(
            [
                last_diag * (STEPS_16 / bound),
                rhs[:, :HALF] * (STEPS_16 / rhs_bound),
                rhs[:, HALF:] * (STEPS_16 / rhs_bound),
                jnp.broadcast_to(bound, (1, HALF)),
                jnp.broadcast_to(rhs_bound, (1, HALF)),
                jnp.zeros((3, HALF), F32),
            ],
            0,
        )
        out_ref[n, K:, :] = jnp.floor(extra + 0.5).astype(jnp.int32).astype(WIRE)


def partial_grams(got):
    return pl.pallas_call(
        gram_kernel,
        grid=(HIGH // PER,),
        in_specs=[
            pl.BlockSpec((GROUP, PER * CAP, K), lambda h: (0, h, 0)),
            pl.BlockSpec((GROUP, 16, K), lambda h: (0, HIGH * CAP // 16, 0)),
        ],
        out_specs=pl.BlockSpec((PER, PACKED, HALF), lambda h: (h, 0, 0)),
        out_shape=jax.ShapeDtypeStruct((HIGH, PACKED, HALF), WIRE),
        name="gram",
        compiler_params=pltpu.CompilerParams(vmem_limit_bytes=16 << 20),
    )(got, got)


def split(a):
    top = a.astype(BF16)
    return top, (a - top.astype(F32)).astype(BF16)


def dot3(a, b):
    (a_top, a_rest), (b_top, b_rest) = a, b
    dot = lambda u, v: jnp.dot(u, v, preferred_element_type=F32)
    return dot(a_top, b_top) + (dot(a_top, b_rest) + dot(a_rest, b_top))


def newton_kernel(got_ref, out_ref):
    packed, rhs_rows = 0.0, 0.0
    for h in range(HIGH):
        coded = got_ref[h].astype(jnp.int32).astype(F32)
        packed += coded * (coded[K + 3 : K + 4] * (1.0 / STEPS_16))
        rhs_rows += coded[K + 1 : K + 3] * (coded[K + 4 : K + 5] * (1.0 / STEPS_16))
    mixed, cross, extra = packed[:HALF], packed[HALF:K], packed[K:]
    low, high = iota((HALF, HALF), 0), iota((HALF, HALF), 1)
    eye = low == high
    base = (K - 1) / inflation
    upper = jnp.where(low < high, mixed, 0.0)
    lower = jnp.where(low > high, mixed, 0.0)
    first_diag = jnp.where(eye, mixed + base, 0.0)
    last_diag = jnp.where(eye, extra[0:1] + base, 0.0)
    first = upper + upper.T + first_diag
    last = lower + lower.T + last_diag
    gram = jnp.concatenate(
        [jnp.concatenate([first, cross], 1), jnp.concatenate([cross.T, last], 1)], 0
    )
    rhs = jnp.concatenate([rhs_rows[0:1], rhs_rows[1:2]], 1)
    total = jnp.sum(jnp.sum(first_diag + last_diag, 1, keepdims=True), 0, keepdims=True)
    identity = (iota((K, K), 0) == iota((K, K), 1)).astype(F32)
    error = gram / total
    root = None
    for step in range(NEWTON_STEPS - 1):
        half = (0.5 * error).astype(BF16)

        def times(*values):
            if step < COARSE_STEPS:
                out = jnp.dot(
                    jnp.concatenate([v.astype(BF16) for v in values], 0), half, preferred_element_type=F32
                )
                return [1.5 * v - out[i * K : (i + 1) * K] for i, v in enumerate(values)]
            parts = [p for v in values for p in split(v)]
            out = jnp.dot(jnp.concatenate(parts, 0), half, preferred_element_type=F32)
            return [
                1.5 * v - (out[2 * i * K : (2 * i + 1) * K] + out[(2 * i + 1) * K : (2 * i + 2) * K])
                for i, v in enumerate(values)
            ]

        if step == 0:
            root = 1.5 * identity - half.astype(F32)
            (error,) = times(error)
        else:
            error, root = times(error, root)
        (error,) = times(error)
    root = 1.5 * root - 0.5 * dot3(split(root), split(error))
    once = jnp.sum(root * rhs, 1, keepdims=True) / total
    mean_weight = jnp.sum(root * once, 0, keepdims=True)
    root = jnp.sqrt((K - 1) / total) * root
    first, last = root[:HALF, :HALF], root[HALF:, HALF:]
    out_ref[:HALF, :] = jnp.where(low < high, first, jnp.where(eye, 0.5 * first, last)).astype(BF16)
    out_ref[HALF:K, :] = root[:HALF, HALF:].astype(BF16)
    weights = [mean_weight[:, :HALF], mean_weight[:, HALF:]]
    tops = [w.astype(BF16).astype(F32) for w in weights]
    last_diag = jnp.sum(jnp.where(eye, 0.5 * last, 0.0), 0, keepdims=True)
    rests = [w - t for w, t in zip(weights, tops)]
    extra = jnp.concatenate([last_diag, *tops, *rests, jnp.zeros((3, HALF), F32)], 0)
    out_ref[K:, :] = extra.astype(BF16)


def node_transform(got):
    return pl.pallas_call(
        newton_kernel,
        out_shape=jax.ShapeDtypeStruct((PACKED, HALF), BF16),
        name="newton",
        compiler_params=pltpu.CompilerParams(vmem_limit_bytes=12 << 20),
    )(got)


def anomaly_kernel(state_ref, anomaly_ref, mean_ref):
    for n in range(COLS):
        state = state_ref[n].astype(F32)
        mean = jnp.mean(state, -1, keepdims=True)
        anomaly_ref[n] = (state - mean).astype(BF16)
        mean_ref[n] = jnp.broadcast_to(mean, mean_ref.shape[1:])


def anomalies(state):
    columns, levels, _ = state.shape
    return pl.pallas_call(
        anomaly_kernel,
        out_shape=[
            jax.ShapeDtypeStruct(state.shape, BF16),
            jax.ShapeDtypeStruct((columns, levels, HALF), F32),
        ],
        name="anomaly",
        cost_estimate=pl.CostEstimate(flops=1 << 21, bytes_accessed=3 << 20, transcendentals=0),
        compiler_params=pltpu.CompilerParams(vmem_limit_bytes=16 << 20),
    )(state)


def analysis_kernel(slot_ref, share_ref, flip_ref, table_ref, anomaly_ref, mean_ref, out_hbm, out_ref, sems):
    copies = []
    flip_x, flip_y = flip_ref[0], flip_ref[1]
    low, high = iota((HALF, HALF), 0), iota((HALF, HALF), 1)
    eye = low == high
    for n in range(COLS):
        cx, cy = n // CY, n % CY
        shares = [share_ref[q, cx, cy] for q in range(4)]
        total = shares[0] + shares[1] + shares[2] + shares[3]
        scale = 1.0 / jnp.full((1, 1), total, F32)
        blend = None
        for q in range(4):
            slot = slot_ref[q, cx, cy]
            ox, oy = slot // 3, slot % 3
            ox = jnp.where(flip_x == 1, ox, 2 - ox)
            oy = jnp.where(flip_y == 1, oy, 2 - oy)
            term = (shares[q] * scale) * table_ref[oy * 3 + ox].astype(F32)
            blend = term if q == 0 else blend + term
        mixed, cross, extra = blend[:HALF], blend[HALF:K], blend[K:]
        upper = jnp.where(low <= high, mixed, 0.0)
        lower = jnp.where(low > high, mixed, jnp.where(eye, extra[0:1], 0.0))
        half = jnp.concatenate(
            [
                jnp.concatenate([upper, cross], 1).astype(BF16),
                jnp.concatenate([jnp.zeros_like(lower), lower], 1).astype(BF16),
            ],
            0,
        )
        weight = jnp.concatenate([extra[1:2] + extra[3:4], extra[2:3] + extra[4:5]], 1)
        top = weight.astype(BF16).astype(F32)
        rows = jnp.concatenate([top, weight - top, jnp.zeros((HALF - 2, K), F32)], 0).astype(BF16)
        anomaly = anomaly_ref[n]
        across = (((1,), (1,)), ((), ()))
        shift = lax.dot_general(anomaly, rows, across, preferred_element_type=F32)
        mean = mean_ref[n] + (shift[:, 0:1] + shift[:, 1:2])
        update = jnp.dot(anomaly, half, preferred_element_type=F32) + lax.dot_general(
            anomaly, half, across, preferred_element_type=F32
        )
        out_ref[n] = (jnp.concatenate([mean, mean], 1) + update).astype(BF16)
        copies.append(pltpu.make_async_copy(out_ref.at[n], out_hbm.at[n], sems.at[n]))
        copies[-1].start()
    for copy in copies:
        copy.wait()


CX = 2
CY = 8
COLS = 16


def analyse(slots, share, flips, table, anomaly, mean):
    columns, levels, width = anomaly.shape
    block = pl.BlockSpec((COLS, levels, width), lambda f, *_: (f, 0, 0))
    wide = pl.BlockSpec((COLS, levels, HALF), lambda f, *_: (f, 0, 0))
    return pl.pallas_call(
        analysis_kernel,
        grid_spec=pltpu.PrefetchScalarGridSpec(
            num_scalar_prefetch=3,
            grid=(columns // COLS,),
            in_specs=[pl.BlockSpec((9, PACKED, HALF), lambda f, *_: (0, 0, 0)), block, wide],
            out_specs=pl.BlockSpec(memory_space=pltpu.HBM),
            scratch_shapes=[pltpu.VMEM((COLS, levels, width), BF16), pltpu.SemaphoreType.DMA((COLS,))],
        ),
        out_shape=jax.ShapeDtypeStruct(anomaly.shape, BF16),
        name="analysis",
        compiler_params=pltpu.CompilerParams(vmem_limit_bytes=16 << 20),
    )(slots, share, flips, table, anomaly, mean)


def swap(block, axes, count):
    even = [(i, i ^ 1) for i in range(count)]
    odd = [(i, (((i + 1) ^ 1) - 1) % count) for i in range(count)]
    far = lax.ppermute(block, axes, odd)
    near = lax.ppermute(block, axes, even)
    return near, far


def shards(members, obs_pert, obs_weight, obs_innov, obs_node, neighbour_slot, interp_weight):
    sent = route(obs_node.reshape(1, OBS), obs_weight, obs_innov, obs_pert[0])
    got = lax.all_to_all(sent, ("x", "zl"), split_axis=0, concat_axis=0, tiled=True)
    grams = partial_grams(got)
    grams = lax.all_to_all(grams, "zh", split_axis=0, concat_axis=0, tiled=True)
    own, members = lax.optimization_barrier((node_transform(grams), members))
    anomaly, mean = anomalies(members.reshape(CX * CY, *members.shape[2:]))
    even, odd = swap(own, GX, 64)
    line = jnp.stack([even, own, odd])
    even, odd = swap(line, GY, 8)
    table = jnp.concatenate([even, line, odd])
    flips = jnp.stack([lax.axis_index(GX) % 2, lax.axis_index(GY) % 2]).astype(jnp.int32)
    return analyse(neighbour_slot, interp_weight, flips, table, anomaly, mean).reshape(members.shape)


def solution(mesh):
    fine = Mesh(mesh.devices.reshape(SHAPE), AXES)
    return jax.shard_map(
        shards,
        mesh=fine,
        in_specs=(
            P(GX, GY, None, None),
            P(GY, GX, None),
            P(GY, GX),
            P(GY, GX),
            P(GY, GX, None),
            P(None, GX, GY),
            P(None, GX, GY),
        ),
        out_specs=P(GX, GY, None, None),
        check_vma=False,
    )
```

```python
import jax
import jax.numpy as jnp
from jax import lax
from jax.experimental import pallas as pl
from jax.experimental.pallas import tpu as pltpu
from jax.sharding import Mesh
from jax.sharding import PartitionSpec as P


NEWTON_STEPS = 8
COARSE_STEPS = 4
inflation = 1.1

SHAPE = (4, 8, 2, 4, 2)
AXES = ("x", "zh", "zl", "y", "c")
GX = ("x", "zh", "zl")
GY = ("y", "c")

NEAR_ORDER = [0, 4, 2, 6, 1, 5, 3, 7]
FAR_ORDER = [0, 4, 2, 6, 1, 5, 3, 7]

NODES = 64
HIGH = 8
GROUP = 8
CAP = 48
DESTS = 8
OBS = 2048
K = 256
HALF = 128
ROWS = HIGH * CAP + 16
PACKED = K + 8
WIRE = jnp.int16
STEPS_16 = 32767.0
F32 = jnp.float32
BF16 = jnp.bfloat16


def iota(shape, dim):
    return lax.broadcasted_iota(jnp.int32, shape, dim)


def route_kernel(
    node_hbm, weight_hbm, innov_hbm, pert_hbm, out_ref,
    rank_ref, scaled_ref, factor_ref, node_ref, weight_ref, innov_ref, pert_ref, sems,
):
    step = pl.program_id(0)

    @pl.when(step == 0)
    def _():
        pairs = (
            (node_hbm, node_ref), (pert_hbm, pert_ref), (weight_hbm, weight_ref), (innov_hbm, innov_ref),
        )
        copies = [pltpu.make_async_copy(a, b, sems.at[i]) for i, (a, b) in enumerate(pairs)]
        for copy in copies:
            copy.start()
        copies[0].wait()
        row = iota((NODES, 1), 0)
        entry = lambda table, at: sum(jnp.where(at == k, v, 0) for k, v in enumerate(table))
        dest = entry(NEAR_ORDER, row // HIGH)
        name = (dest // 2) * 16 + entry(FAR_ORDER, row % HIGH) * 2 + dest % 2
        onehot = (node_ref[...] == name).astype(F32)
        upper = (iota((K, K), 0) <= iota((K, K), 1)).astype(BF16)
        blocks = [onehot[:, b * K : (b + 1) * K] for b in range(OBS // K)]
        counts = jnp.dot(
            jnp.concatenate(blocks, 0).astype(BF16), upper, preferred_element_type=F32
        )
        carry = jnp.zeros((NODES, 1), F32)
        for b, block in enumerate(blocks):
            count = counts[b * NODES : (b + 1) * NODES]
            rank_ref[:, b * K : (b + 1) * K] = jnp.where(block > 0, count + (carry - 1.0), -1.0)
            carry += count[:, K - 1 : K]
        for copy in copies[1:]:
            copy.wait()
        side = jnp.sqrt(weight_ref[...].astype(F32))
        factor = onehot * (side * innov_ref[...].astype(F32))
        top = factor.astype(BF16)
        factor_ref[:NODES, :] = top
        factor_ref[NODES:, :] = (factor - top.astype(F32)).astype(BF16)
        side = jnp.concatenate([side[:, k * 128 : (k + 1) * 128] for k in range(OBS // 128)], 0).T
        for k in range(OBS // 128):
            rows = pl.ds(k * 128, 128)
            scaled_ref[rows, :] = (pert_ref[rows, :].astype(F32) * side[:, k : k + 1]).astype(BF16)

    rows = pl.ds(pl.multiple_of(step * DESTS * HIGH, DESTS * HIGH), DESTS * HIGH)
    more = pl.ds(pl.multiple_of(NODES + step * DESTS * HIGH, DESTS * HIGH), DESTS * HIGH)
    rank = rank_ref[rows, :]
    wanted = iota((CAP, OBS), 0).astype(F32)
    pick = jnp.concatenate(
        [(rank[h : h + 1, :] == wanted).astype(BF16) for h in range(DESTS * HIGH)]
        + [factor_ref[rows, :], factor_ref[more, :]],
        0,
    )
    picked = jnp.dot(pick, scaled_ref[...], preferred_element_type=F32)
    count = DESTS * HIGH
    rhs = picked[count * CAP : count * CAP + count] + picked[count * CAP + count :]
    picked = picked[: count * CAP].astype(BF16)
    top = rhs.astype(BF16).astype(F32)
    rest = rhs - top
    for d in range(DESTS):
        out_ref[d, : HIGH * CAP, :] = picked[d * HIGH * CAP : (d + 1) * HIGH * CAP]
        mine = slice(d * HIGH, (d + 1) * HIGH)
        out_ref[d, HIGH * CAP :, :] = jnp.concatenate([top[mine], rest[mine]], 0).astype(BF16)


def route(node, weight, innov, pert):
    return pl.pallas_call(
        route_kernel,
        grid=(GROUP // DESTS,),
        in_specs=[pl.BlockSpec(memory_space=pltpu.HBM)] * 4,
        out_specs=pl.BlockSpec((DESTS, ROWS, K), lambda d: (d, 0, 0)),
        out_shape=jax.ShapeDtypeStruct((GROUP, ROWS, K), BF16),
        scratch_shapes=[
            pltpu.VMEM((NODES, OBS), F32),
            pltpu.VMEM((OBS, K), BF16),
            pltpu.VMEM((2 * NODES, OBS), BF16),
            pltpu.VMEM((1, OBS), jnp.int32),
            pltpu.VMEM((1, OBS), BF16),
            pltpu.VMEM((1, OBS), BF16),
            pltpu.VMEM((OBS, K), BF16),
            pltpu.SemaphoreType.DMA((4,)),
        ],
        name="route",
        compiler_params=pltpu.CompilerParams(vmem_limit_bytes=40 << 20),
    )(*[pltpu.with_memory_space_constraint(v, pltpu.HBM) for v in (node, weight, innov, pert)])


PER = 2


def code(value, bound):
    scaled = jnp.floor(value * (STEPS_16 / bound) + 0.5)
    return scaled.astype(jnp.int32).astype(WIRE)


def bound_of(value):
    most = jnp.max(jnp.max(jnp.abs(value), 1, keepdims=True), 0, keepdims=True)
    return jnp.floor(most) + 1.0


def gram_kernel(obs_ref, side_ref, out_ref):
    step = pl.program_id(0)
    low, high = iota((HALF, HALF), 0), iota((HALF, HALF), 1)
    eye = low == high
    keep = low <= high
    sides = jnp.sum(side_ref[...].astype(F32), 0)
    name = iota((16, K), 0) % HIGH
    for n in range(PER):
        obs = obs_ref[:, n * CAP : (n + 1) * CAP, :].reshape(GROUP * CAP, K)
        gram = lax.dot_general(obs, obs, (((0,), (0,)), ((), ())), preferred_element_type=F32)
        first, cross, last = gram[:HALF, :HALF], gram[:HALF, HALF:], gram[HALF:, HALF:]
        first_diag = jnp.sum(jnp.where(eye, first, 0.0), 0, keepdims=True)
        last_diag = jnp.sum(jnp.where(eye, last, 0.0), 0, keepdims=True)
        rhs = jnp.sum(jnp.where(name == step * PER + n, sides, 0.0), 0, keepdims=True)
        bound = bound_of(jnp.maximum(first_diag, last_diag))
        rhs_bound = bound_of(rhs)
        out_ref[n, :HALF, :] = code(jnp.where(keep, first, last), bound)
        out_ref[n, HALF:K, :] = code(cross, bound)
        extra = jnp.concatenate(
            [
                last_diag * (STEPS_16 / bound),
                rhs[:, :HALF] * (STEPS_16 / rhs_bound),
                rhs[:, HALF:] * (STEPS_16 / rhs_bound),
                jnp.broadcast_to(bound, (1, HALF)),
                jnp.broadcast_to(rhs_bound, (1, HALF)),
                jnp.zeros((3, HALF), F32),
            ],
            0,
        )
        out_ref[n, K:, :] = jnp.floor(extra + 0.5).astype(jnp.int32).astype(WIRE)


def partial_grams(got):
    return pl.pallas_call(
        gram_kernel,
        grid=(HIGH // PER,),
        in_specs=[
            pl.BlockSpec((GROUP, PER * CAP, K), lambda h: (0, h, 0)),
            pl.BlockSpec((GROUP, 16, K), lambda h: (0, HIGH * CAP // 16, 0)),
        ],
        out_specs=pl.BlockSpec((PER, PACKED, HALF), lambda h: (h, 0, 0)),
        out_shape=jax.ShapeDtypeStruct((HIGH, PACKED, HALF), WIRE),
        name="gram",
        compiler_params=pltpu.CompilerParams(vmem_limit_bytes=16 << 20),
    )(got, got)


def split(a):
    top = a.astype(BF16)
    return top, (a - top.astype(F32)).astype(BF16)


def dot3(a, b):
    (a_top, a_rest), (b_top, b_rest) = a, b
    dot = lambda u, v: jnp.dot(u, v, preferred_element_type=F32)
    return dot(a_top, b_top) + (dot(a_top, b_rest) + dot(a_rest, b_top))


def newton_kernel(got_ref, out_ref):
    packed, rhs_rows = 0.0, 0.0
    for h in range(HIGH):
        coded = got_ref[h].astype(jnp.int32).astype(F32)
        packed += coded * (coded[K + 3 : K + 4] * (1.0 / STEPS_16))
        rhs_rows += coded[K + 1 : K + 3] * (coded[K + 4 : K + 5] * (1.0 / STEPS_16))
    mixed, cross, extra = packed[:HALF], packed[HALF:K], packed[K:]
    low, high = iota((HALF, HALF), 0), iota((HALF, HALF), 1)
    eye = low == high
    base = (K - 1) / inflation
    upper = jnp.where(low < high, mixed, 0.0)
    lower = jnp.where(low > high, mixed, 0.0)
    first_diag = jnp.where(eye, mixed + base, 0.0)
    last_diag = jnp.where(eye, extra[0:1] + base, 0.0)
    first = upper + upper.T + first_diag
    last = lower + lower.T + last_diag
    gram = jnp.concatenate(
        [jnp.concatenate([first, cross], 1), jnp.concatenate([cross.T, last], 1)], 0
    )
    rhs = jnp.concatenate([rhs_rows[0:1], rhs_rows[1:2]], 1)
    total = jnp.sum(jnp.sum(first_diag + last_diag, 1, keepdims=True), 0, keepdims=True)
    identity = (iota((K, K), 0) == iota((K, K), 1)).astype(F32)
    error = gram / total
    root = None
    for step in range(NEWTON_STEPS - 1):
        half = (0.5 * error).astype(BF16)

        def times(*values):
            if step < COARSE_STEPS:
                out = jnp.dot(
                    jnp.concatenate([v.astype(BF16) for v in values], 0), half, preferred_element_type=F32
                )
                return [1.5 * v - out[i * K : (i + 1) * K] for i, v in enumerate(values)]
            parts = [p for v in values for p in split(v)]
            out = jnp.dot(jnp.concatenate(parts, 0), half, preferred_element_type=F32)
            return [
                1.5 * v - (out[2 * i * K : (2 * i + 1) * K] + out[(2 * i + 1) * K : (2 * i + 2) * K])
                for i, v in enumerate(values)
            ]

        if step == 0:
            root = 1.5 * identity - half.astype(F32)
            (error,) = times(error)
        else:
            error, root = times(error, root)
        (error,) = times(error)
    root = 1.5 * root - 0.5 * dot3(split(root), split(error))
    once = jnp.sum(root * rhs, 1, keepdims=True) / total
    mean_weight = jnp.sum(root * once, 0, keepdims=True)
    root = jnp.sqrt((K - 1) / total) * root
    first, last = root[:HALF, :HALF], root[HALF:, HALF:]
    out_ref[:HALF, :] = jnp.where(low < high, first, jnp.where(eye, 0.5 * first, last)).astype(BF16)
    out_ref[HALF:K, :] = root[:HALF, HALF:].astype(BF16)
    weights = [mean_weight[:, :HALF], mean_weight[:, HALF:]]
    tops = [w.astype(BF16).astype(F32) for w in weights]
    last_diag = jnp.sum(jnp.where(eye, 0.5 * last, 0.0), 0, keepdims=True)
    rests = [w - t for w, t in zip(weights, tops)]
    extra = jnp.concatenate([last_diag, *tops, *rests, jnp.zeros((3, HALF), F32)], 0)
    out_ref[K:, :] = extra.astype(BF16)


def node_transform(got):
    return pl.pallas_call(
        newton_kernel,
        out_shape=jax.ShapeDtypeStruct((PACKED, HALF), BF16),
        name="newton",
        compiler_params=pltpu.CompilerParams(vmem_limit_bytes=12 << 20),
    )(got)


def anomaly_kernel(state_ref, anomaly_ref, mean_ref):
    for n in range(COLS):
        state = state_ref[n].astype(F32)
        mean = jnp.mean(state, -1, keepdims=True)
        anomaly_ref[n] = (state - mean).astype(BF16)
        mean_ref[n] = jnp.broadcast_to(mean, mean_ref.shape[1:])


def anomalies(state):
    columns, levels, _ = state.shape
    return pl.pallas_call(
        anomaly_kernel,
        out_shape=[
            jax.ShapeDtypeStruct(state.shape, BF16),
            jax.ShapeDtypeStruct((columns, levels, HALF), F32),
        ],
        name="anomaly",
        cost_estimate=pl.CostEstimate(flops=1 << 21, bytes_accessed=3 << 20, transcendentals=0),
        compiler_params=pltpu.CompilerParams(vmem_limit_bytes=16 << 20),
    )(state)


def analysis_kernel(slot_ref, share_ref, flip_ref, table_ref, anomaly_ref, mean_ref, out_hbm, out_ref, sems):
    copies = []
    flip_x, flip_y = flip_ref[0], flip_ref[1]
    low, high = iota((HALF, HALF), 0), iota((HALF, HALF), 1)
    eye = low == high
    for n in range(COLS):
        cx, cy = n // CY, n % CY
        shares = [share_ref[q, cx, cy] for q in range(4)]
        total = shares[0] + shares[1] + shares[2] + shares[3]
        scale = 1.0 / jnp.full((1, 1), total, F32)
        blend = None
        for q in range(4):
            slot = slot_ref[q, cx, cy]
            ox, oy = slot // 3, slot % 3
            ox = jnp.where(flip_x == 1, ox, 2 - ox)
            oy = jnp.where(flip_y == 1, oy, 2 - oy)
            term = (shares[q] * scale) * table_ref[oy * 3 + ox].astype(F32)
            blend = term if q == 0 else blend + term
        mixed, cross, extra = blend[:HALF], blend[HALF:K], blend[K:]
        upper = jnp.where(low <= high, mixed, 0.0)
        lower = jnp.where(low > high, mixed, jnp.where(eye, extra[0:1], 0.0))
        half = jnp.concatenate(
            [
                jnp.concatenate([upper, cross], 1).astype(BF16),
                jnp.concatenate([jnp.zeros_like(lower), lower], 1).astype(BF16),
            ],
            0,
        )
        weight = jnp.concatenate([extra[1:2] + extra[3:4], extra[2:3] + extra[4:5]], 1)
        top = weight.astype(BF16).astype(F32)
        rows = jnp.concatenate([top, weight - top, jnp.zeros((HALF - 2, K), F32)], 0).astype(BF16)
        anomaly = anomaly_ref[n]
        across = (((1,), (1,)), ((), ()))
        shift = lax.dot_general(anomaly, rows, across, preferred_element_type=F32)
        mean = mean_ref[n] + (shift[:, 0:1] + shift[:, 1:2])
        update = jnp.dot(anomaly, half, preferred_element_type=F32) + lax.dot_general(
            anomaly, half, across, preferred_element_type=F32
        )
        out_ref[n] = (jnp.concatenate([mean, mean], 1) + update).astype(BF16)
        copies.append(pltpu.make_async_copy(out_ref.at[n], out_hbm.at[n], sems.at[n]))
        copies[-1].start()
    for copy in copies:
        copy.wait()


CX = 2
CY = 8
COLS = 16


def analyse(slots, share, flips, table, anomaly, mean):
    columns, levels, width = anomaly.shape
    block = pl.BlockSpec((COLS, levels, width), lambda f, *_: (f, 0, 0))
    wide = pl.BlockSpec((COLS, levels, HALF), lambda f, *_: (f, 0, 0))
    return pl.pallas_call(
        analysis_kernel,
        grid_spec=pltpu.PrefetchScalarGridSpec(
            num_scalar_prefetch=3,
            grid=(columns // COLS,),
            in_specs=[pl.BlockSpec((9, PACKED, HALF), lambda f, *_: (0, 0, 0)), block, wide],
            out_specs=pl.BlockSpec(memory_space=pltpu.HBM),
            scratch_shapes=[pltpu.VMEM((COLS, levels, width), BF16), pltpu.SemaphoreType.DMA((COLS,))],
        ),
        out_shape=jax.ShapeDtypeStruct(anomaly.shape, BF16),
        name="analysis",
        compiler_params=pltpu.CompilerParams(vmem_limit_bytes=16 << 20),
    )(slots, share, flips, table, anomaly, mean)


def swap(block, axes, count):
    even = [(i, i ^ 1) for i in range(count)]
    odd = [(i, (((i + 1) ^ 1) - 1) % count) for i in range(count)]
    far = lax.ppermute(block, axes, odd)
    near = lax.ppermute(block, axes, even)
    return near, far


def shards(members, obs_pert, obs_weight, obs_innov, obs_node, neighbour_slot, interp_weight):
    sent = route(obs_node.reshape(1, OBS), obs_weight, obs_innov, obs_pert[0])
    got = lax.all_to_all(
        sent, ("x", "zl"), split_axis=0, concat_axis=0, tiled=True, axis_index_groups=[NEAR_ORDER]
    )
    grams = partial_grams(got)
    grams = lax.all_to_all(
        grams, "zh", split_axis=0, concat_axis=0, tiled=True, axis_index_groups=[FAR_ORDER]
    )
    own, members = lax.optimization_barrier((node_transform(grams), members))
    anomaly, mean = anomalies(members.reshape(CX * CY, *members.shape[2:]))
    even, odd = swap(own, GX, 64)
    line = jnp.stack([even, own, odd])
    even, odd = swap(line, GY, 8)
    table = jnp.concatenate([even, line, odd])
    flips = jnp.stack([lax.axis_index(GX) % 2, lax.axis_index(GY) % 2]).astype(jnp.int32)
    return analyse(neighbour_slot, interp_weight, flips, table, anomaly, mean).reshape(members.shape)


def solution(mesh):
    fine = Mesh(mesh.devices.reshape(SHAPE), AXES)
    return jax.shard_map(
        shards,
        mesh=fine,
        in_specs=(
            P(GX, GY, None, None),
            P(GY, GX, None),
            P(GY, GX),
            P(GY, GX),
            P(GY, GX, None),
            P(None, GX, GY),
            P(None, GX, GY),
        ),
        out_specs=P(GX, GY, None, None),
        check_vma=False,
    )
```

```python
import jax
import jax.numpy as jnp
from jax import lax
from jax.experimental import pallas as pl
from jax.experimental.pallas import tpu as pltpu
from jax.sharding import Mesh
from jax.sharding import PartitionSpec as P


NEWTON_STEPS = 8
COARSE_STEPS = 4
inflation = 1.1

SHAPE = (4, 8, 2, 4, 2)
AXES = ("x", "zh", "zl", "y", "c")
GX = ("x", "zh", "zl")
GY = ("y", "c")

NEAR_ORDER = [0, 4, 2, 6, 1, 5, 3, 7]
FAR_ORDER = [0, 4, 2, 6, 1, 5, 3, 7]

NODES = 64
HIGH = 8
GROUP = 8
CAP = 48
DESTS = 8
OBS = 2048
K = 256
HALF = 128
ROWS = HIGH * CAP + 16
PACKED = K + 8
WIRE = jnp.int16
STEPS_16 = 32767.0
F32 = jnp.float32
BF16 = jnp.bfloat16


def iota(shape, dim):
    return lax.broadcasted_iota(jnp.int32, shape, dim)


def route_kernel(
    node_hbm, weight_hbm, innov_hbm, pert_hbm, out_ref,
    rank_ref, scaled_ref, factor_ref, node_ref, weight_ref, innov_ref, pert_ref, sems,
):
    step = pl.program_id(0)

    @pl.when(step == 0)
    def _():
        pairs = (
            (node_hbm, node_ref), (pert_hbm, pert_ref), (weight_hbm, weight_ref), (innov_hbm, innov_ref),
        )
        copies = [pltpu.make_async_copy(a, b, sems.at[i]) for i, (a, b) in enumerate(pairs)]
        for copy in copies:
            copy.start()
        copies[0].wait()
        row = iota((NODES, 1), 0)
        entry = lambda table, at: sum(jnp.where(at == k, v, 0) for k, v in enumerate(table))
        dest = entry(NEAR_ORDER, row // HIGH)
        name = (dest // 2) * 16 + entry(FAR_ORDER, row % HIGH) * 2 + dest % 2
        onehot = (node_ref[...] == name).astype(F32)
        upper = (iota((K, K), 0) <= iota((K, K), 1)).astype(BF16)
        blocks = [onehot[:, b * K : (b + 1) * K] for b in range(OBS // K)]
        counts = jnp.dot(
            jnp.concatenate(blocks, 0).astype(BF16), upper, preferred_element_type=F32
        )
        carry = jnp.zeros((NODES, 1), F32)
        for b, block in enumerate(blocks):
            count = counts[b * NODES : (b + 1) * NODES]
            rank_ref[:, b * K : (b + 1) * K] = jnp.where(block > 0, count + (carry - 1.0), -1.0)
            carry += count[:, K - 1 : K]
        for copy in copies[1:]:
            copy.wait()
        side = jnp.sqrt(weight_ref[...].astype(F32))
        factor = onehot * (side * innov_ref[...].astype(F32))
        top = factor.astype(BF16)
        factor_ref[:NODES, :] = top
        factor_ref[NODES:, :] = (factor - top.astype(F32)).astype(BF16)
        side = jnp.concatenate([side[:, k * 128 : (k + 1) * 128] for k in range(OBS // 128)], 0).T
        for k in range(OBS // 128):
            rows = pl.ds(k * 128, 128)
            scaled_ref[rows, :] = (pert_ref[rows, :].astype(F32) * side[:, k : k + 1]).astype(BF16)

    rows = pl.ds(pl.multiple_of(step * DESTS * HIGH, DESTS * HIGH), DESTS * HIGH)
    more = pl.ds(pl.multiple_of(NODES + step * DESTS * HIGH, DESTS * HIGH), DESTS * HIGH)
    rank = rank_ref[rows, :]
    wanted = iota((CAP, OBS), 0).astype(F32)
    pick = jnp.concatenate(
        [(rank[h : h + 1, :] == wanted).astype(BF16) for h in range(DESTS * HIGH)]
        + [factor_ref[rows, :], factor_ref[more, :]],
        0,
    )
    picked = jnp.dot(pick, scaled_ref[...], preferred_element_type=F32)
    count = DESTS * HIGH
    rhs = picked[count * CAP : count * CAP + count] + picked[count * CAP + count :]
    picked = picked[: count * CAP].astype(BF16)
    top = rhs.astype(BF16).astype(F32)
    rest = rhs - top
    for d in range(DESTS):
        out_ref[d, : HIGH * CAP, :] = picked[d * HIGH * CAP : (d + 1) * HIGH * CAP]
        mine = slice(d * HIGH, (d + 1) * HIGH)
        out_ref[d, HIGH * CAP :, :] = jnp.concatenate([top[mine], rest[mine]], 0).astype(BF16)


def route(node, weight, innov, pert):
    return pl.pallas_call(
        route_kernel,
        grid=(GROUP // DESTS,),
        in_specs=[pl.BlockSpec(memory_space=pltpu.HBM)] * 4,
        out_specs=pl.BlockSpec((DESTS, ROWS, K), lambda d: (d, 0, 0)),
        out_shape=jax.ShapeDtypeStruct((GROUP, ROWS, K), BF16),
        scratch_shapes=[
            pltpu.VMEM((NODES, OBS), F32),
            pltpu.VMEM((OBS, K), BF16),
            pltpu.VMEM((2 * NODES, OBS), BF16),
            pltpu.VMEM((1, OBS), jnp.int32),
            pltpu.VMEM((1, OBS), BF16),
            pltpu.VMEM((1, OBS), BF16),
            pltpu.VMEM((OBS, K), BF16),
            pltpu.SemaphoreType.DMA((4,)),
        ],
        name="route",
        compiler_params=pltpu.CompilerParams(vmem_limit_bytes=40 << 20),
    )(*[pltpu.with_memory_space_constraint(v, pltpu.HBM) for v in (node, weight, innov, pert)])


PER = 4


def code(value, bound):
    return jnp.round(value * (STEPS_16 / bound)).astype(jnp.int32).astype(WIRE)


def bound_of(value):
    most = jnp.max(jnp.max(jnp.abs(value), 1, keepdims=True), 0, keepdims=True)
    return jnp.floor(most) + 1.0


def gram_kernel(obs_ref, side_ref, out_ref):
    step = pl.program_id(0)
    low, high = iota((HALF, HALF), 0), iota((HALF, HALF), 1)
    eye = low == high
    keep = low <= high
    sides = jnp.sum(side_ref[...].astype(F32), 0)
    name = iota((16, K), 0) % HIGH
    for n in range(PER):
        obs = obs_ref[:, n * CAP : (n + 1) * CAP, :].reshape(GROUP * CAP, K)
        gram = lax.dot_general(obs, obs, (((0,), (0,)), ((), ())), preferred_element_type=F32)
        first, cross, last = gram[:HALF, :HALF], gram[:HALF, HALF:], gram[HALF:, HALF:]
        first_diag = jnp.sum(jnp.where(eye, first, 0.0), 0, keepdims=True)
        last_diag = jnp.sum(jnp.where(eye, last, 0.0), 0, keepdims=True)
        rhs = jnp.sum(jnp.where(name == step * PER + n, sides, 0.0), 0, keepdims=True)
        bound = bound_of(jnp.maximum(first_diag, last_diag))
        rhs_bound = bound_of(rhs)
        out_ref[n, :HALF, :] = code(jnp.where(keep, first, last), bound)
        out_ref[n, HALF:K, :] = code(cross, bound)
        extra = jnp.concatenate(
            [
                last_diag * (STEPS_16 / bound),
                rhs[:, :HALF] * (STEPS_16 / rhs_bound),
                rhs[:, HALF:] * (STEPS_16 / rhs_bound),
                jnp.broadcast_to(bound, (1, HALF)),
                jnp.broadcast_to(rhs_bound, (1, HALF)),
                jnp.zeros((3, HALF), F32),
            ],
            0,
        )
        out_ref[n, K:, :] = jnp.floor(extra + 0.5).astype(jnp.int32).astype(WIRE)


def partial_grams(got):
    return pl.pallas_call(
        gram_kernel,
        grid=(HIGH // PER,),
        in_specs=[
            pl.BlockSpec((GROUP, PER * CAP, K), lambda h: (0, h, 0)),
            pl.BlockSpec((GROUP, 16, K), lambda h: (0, HIGH * CAP // 16, 0)),
        ],
        out_specs=pl.BlockSpec((PER, PACKED, HALF), lambda h: (h, 0, 0)),
        out_shape=jax.ShapeDtypeStruct((HIGH, PACKED, HALF), WIRE),
        name="gram",
        compiler_params=pltpu.CompilerParams(vmem_limit_bytes=16 << 20),
    )(got, got)


def split(a):
    top = a.astype(BF16)
    return top, (a - top.astype(F32)).astype(BF16)


def dot3(a, b):
    (a_top, a_rest), (b_top, b_rest) = a, b
    dot = lambda u, v: jnp.dot(u, v, preferred_element_type=F32)
    return dot(a_top, b_top) + (dot(a_top, b_rest) + dot(a_rest, b_top))


def newton_kernel(got_ref, out_ref):
    packed, rhs_rows = 0.0, 0.0
    for h in range(HIGH):
        coded = got_ref[h].astype(jnp.int32).astype(F32)
        packed += coded * (coded[K + 3 : K + 4] * (1.0 / STEPS_16))
        rhs_rows += coded[K + 1 : K + 3] * (coded[K + 4 : K + 5] * (1.0 / STEPS_16))
    mixed, cross, extra = packed[:HALF], packed[HALF:K], packed[K:]
    low, high = iota((HALF, HALF), 0), iota((HALF, HALF), 1)
    eye = low == high
    base = (K - 1) / inflation
    upper = jnp.where(low < high, mixed, 0.0)
    lower = jnp.where(low > high, mixed, 0.0)
    first_diag = jnp.where(eye, mixed + base, 0.0)
    last_diag = jnp.where(eye, extra[0:1] + base, 0.0)
    first = upper + upper.T + first_diag
    last = lower + lower.T + last_diag
    gram = jnp.concatenate(
        [jnp.concatenate([first, cross], 1), jnp.concatenate([cross.T, last], 1)], 0
    )
    rhs = jnp.concatenate([rhs_rows[0:1], rhs_rows[1:2]], 1)
    total = jnp.sum(jnp.sum(first_diag + last_diag, 1, keepdims=True), 0, keepdims=True)
    identity = (iota((K, K), 0) == iota((K, K), 1)).astype(F32)
    error = gram / total
    root = None
    for step in range(NEWTON_STEPS - 1):
        half = (0.5 * error).astype(BF16)

        def times(*values):
            if step < COARSE_STEPS:
                out = jnp.dot(
                    jnp.concatenate([v.astype(BF16) for v in values], 0), half, preferred_element_type=F32
                )
                return [1.5 * v - out[i * K : (i + 1) * K] for i, v in enumerate(values)]
            parts = [p for v in values for p in split(v)]
            out = jnp.dot(jnp.concatenate(parts, 0), half, preferred_element_type=F32)
            return [
                1.5 * v - (out[2 * i * K : (2 * i + 1) * K] + out[(2 * i + 1) * K : (2 * i + 2) * K])
                for i, v in enumerate(values)
            ]

        if step == 0:
            root = 1.5 * identity - half.astype(F32)
            (error,) = times(error)
        else:
            error, root = times(error, root)
        (error,) = times(error)
    root = 1.5 * root - 0.5 * dot3(split(root), split(error))
    once = jnp.sum(root * rhs, 1, keepdims=True) / total
    mean_weight = jnp.sum(root * once, 0, keepdims=True)
    root = jnp.sqrt((K - 1) / total) * root
    first, last = root[:HALF, :HALF], root[HALF:, HALF:]
    out_ref[:HALF, :] = jnp.where(low < high, first, jnp.where(eye, 0.5 * first, last)).astype(BF16)
    out_ref[HALF:K, :] = root[:HALF, HALF:].astype(BF16)
    weights = [mean_weight[:, :HALF], mean_weight[:, HALF:]]
    tops = [w.astype(BF16).astype(F32) for w in weights]
    last_diag = jnp.sum(jnp.where(eye, 0.5 * last, 0.0), 0, keepdims=True)
    rests = [w - t for w, t in zip(weights, tops)]
    extra = jnp.concatenate([last_diag, *tops, *rests, jnp.zeros((3, HALF), F32)], 0)
    out_ref[K:, :] = extra.astype(BF16)


def node_transform(got):
    return pl.pallas_call(
        newton_kernel,
        out_shape=jax.ShapeDtypeStruct((PACKED, HALF), BF16),
        name="newton",
        compiler_params=pltpu.CompilerParams(vmem_limit_bytes=12 << 20),
    )(got)


def anomaly_kernel(state_ref, anomaly_ref, mean_ref):
    for n in range(COLS):
        state = state_ref[n].astype(F32)
        mean = jnp.mean(state, -1, keepdims=True)
        anomaly_ref[n] = (state - mean).astype(BF16)
        mean_ref[n] = jnp.broadcast_to(mean, mean_ref.shape[1:])


def anomalies(state):
    columns, levels, _ = state.shape
    return pl.pallas_call(
        anomaly_kernel,
        out_shape=[
            jax.ShapeDtypeStruct(state.shape, BF16),
            jax.ShapeDtypeStruct((columns, levels, HALF), F32),
        ],
        name="anomaly",
        cost_estimate=pl.CostEstimate(flops=1 << 21, bytes_accessed=3 << 20, transcendentals=0),
        compiler_params=pltpu.CompilerParams(vmem_limit_bytes=16 << 20),
    )(state)


def analysis_kernel(slot_ref, share_ref, flip_ref, table_ref, anomaly_ref, mean_ref, out_hbm, out_ref, sems):
    copies = []
    flip_x, flip_y = flip_ref[0], flip_ref[1]
    low, high = iota((HALF, HALF), 0), iota((HALF, HALF), 1)
    eye = low == high
    for n in range(COLS):
        cx, cy = n // CY, n % CY
        shares = [share_ref[q, cx, cy] for q in range(4)]
        total = shares[0] + shares[1] + shares[2] + shares[3]
        scale = 1.0 / jnp.full((1, 1), total, F32)
        blend = None
        for q in range(4):
            slot = slot_ref[q, cx, cy]
            ox, oy = slot // 3, slot % 3
            ox = jnp.where(flip_x == 1, ox, 2 - ox)
            oy = jnp.where(flip_y == 1, oy, 2 - oy)
            term = (shares[q] * scale) * table_ref[oy * 3 + ox].astype(F32)
            blend = term if q == 0 else blend + term
        mixed, cross, extra = blend[:HALF], blend[HALF:K], blend[K:]
        upper = jnp.where(low <= high, mixed, 0.0)
        lower = jnp.where(low > high, mixed, jnp.where(eye, extra[0:1], 0.0))
        half = jnp.concatenate(
            [
                jnp.concatenate([upper, cross], 1).astype(BF16),
                jnp.concatenate([jnp.zeros_like(lower), lower], 1).astype(BF16),
            ],
            0,
        )
        weight = jnp.concatenate([extra[1:2] + extra[3:4], extra[2:3] + extra[4:5]], 1)
        top = weight.astype(BF16).astype(F32)
        rows = jnp.concatenate([top, weight - top, jnp.zeros((HALF - 2, K), F32)], 0).astype(BF16)
        anomaly = anomaly_ref[n]
        across = (((1,), (1,)), ((), ()))
        shift = lax.dot_general(anomaly, rows, across, preferred_element_type=F32)
        mean = mean_ref[n] + (shift[:, 0:1] + shift[:, 1:2])
        update = jnp.dot(anomaly, half, preferred_element_type=F32) + lax.dot_general(
            anomaly, half, across, preferred_element_type=F32
        )
        out_ref[n] = (jnp.concatenate([mean, mean], 1) + update).astype(BF16)
        copies.append(pltpu.make_async_copy(out_ref.at[n], out_hbm.at[n], sems.at[n]))
        copies[-1].start()
    for copy in copies:
        copy.wait()


CX = 2
CY = 8
COLS = 16


def analyse(slots, share, flips, table, anomaly, mean):
    columns, levels, width = anomaly.shape
    block = pl.BlockSpec((COLS, levels, width), lambda f, *_: (f, 0, 0))
    wide = pl.BlockSpec((COLS, levels, HALF), lambda f, *_: (f, 0, 0))
    return pl.pallas_call(
        analysis_kernel,
        grid_spec=pltpu.PrefetchScalarGridSpec(
            num_scalar_prefetch=3,
            grid=(columns // COLS,),
            in_specs=[pl.BlockSpec((9, PACKED, HALF), lambda f, *_: (0, 0, 0)), block, wide],
            out_specs=pl.BlockSpec(memory_space=pltpu.HBM),
            scratch_shapes=[pltpu.VMEM((COLS, levels, width), BF16), pltpu.SemaphoreType.DMA((COLS,))],
        ),
        out_shape=jax.ShapeDtypeStruct(anomaly.shape, BF16),
        name="analysis",
        compiler_params=pltpu.CompilerParams(vmem_limit_bytes=16 << 20),
    )(slots, share, flips, table, anomaly, mean)


def swap(block, axes, count):
    even = [(i, i ^ 1) for i in range(count)]
    odd = [(i, (((i + 1) ^ 1) - 1) % count) for i in range(count)]
    far = lax.ppermute(block, axes, odd)
    near = lax.ppermute(block, axes, even)
    return near, far


def shards(members, obs_pert, obs_weight, obs_innov, obs_node, neighbour_slot, interp_weight):
    sent = route(obs_node.reshape(1, OBS), obs_weight, obs_innov, obs_pert[0])
    got = lax.all_to_all(
        sent, ("x", "zl"), split_axis=0, concat_axis=0, tiled=True, axis_index_groups=[NEAR_ORDER]
    )
    grams = partial_grams(got)
    grams = lax.all_to_all(
        grams, "zh", split_axis=0, concat_axis=0, tiled=True, axis_index_groups=[FAR_ORDER]
    )
    own, members = lax.optimization_barrier((node_transform(grams), members))
    anomaly, mean = anomalies(members.reshape(CX * CY, *members.shape[2:]))
    even, odd = swap(own, GX, 64)
    line = jnp.stack([even, own, odd])
    even, odd = swap(line, GY, 8)
    table = jnp.concatenate([even, line, odd])
    flips = jnp.stack([lax.axis_index(GX) % 2, lax.axis_index(GY) % 2]).astype(jnp.int32)
    return analyse(neighbour_slot, interp_weight, flips, table, anomaly, mean).reshape(members.shape)


def solution(mesh):
    fine = Mesh(mesh.devices.reshape(SHAPE), AXES)
    return jax.shard_map(
        shards,
        mesh=fine,
        in_specs=(
            P(GX, GY, None, None),
            P(GY, GX, None),
            P(GY, GX),
            P(GY, GX),
            P(GY, GX, None),
            P(None, GX, GY),
            P(None, GX, GY),
        ),
        out_specs=P(GX, GY, None, None),
        check_vma=False,
    )
```
